32 devices in a mesh: tm: 8 (over y, x, core), seq: 4 (over z).
Axes of the slice: x: 2, y: 2, z: 4, core: 2. Of those that a mesh axis runs over, the one named last changes fastest.
Arguments:
- latents: bfloat16 [32, 16, 2048], P('tm', None, 'seq'), may hold values from -6 to 6
- hidden: bfloat16 [16384, 3072], P(('tm', 'seq')), may hold values from -6 to 6
- grad_out: bfloat16 [32, 512, 2048], P('tm', None, 'seq'), may hold values from -6 to 6
- conv_in_w: bfloat16 [3, 512, 16], replicated, may hold values from -0.875 to 0.875
- conv_in_b: float32 [512], replicated, may hold values from -4 to 4
- conv_w: bfloat16 [3, 512, 512], replicated, may hold values from -0.15625 to 0.15625
- final_w: bfloat16 [3072, 64], replicated, may hold values from -0.109375 to 0.109375
- modulation: float32 [2, 3072], replicated, may hold values from -3 to 3
- clip_start: int32 [32], replicated, may hold values from 0 to 31, as said below
Outputs:
- hidden_input_gradient: bfloat16 [16384, 3072], P(('tm', 'seq'))
- convolution_weight_gradient: float32 [512, 3, 512], P(('tm', 'seq'))
- input_convolution_gradient: float32 [3, 512, 16], replicated
- input_bias_gradient: float32 [512], replicated
- final_grad: float32 [3072, 64], replicated
- modulation_grad: float32 [2, 3072], replicated
The draws below stay inside these ranges and needn't reach their ends.
Inputs may be any that keep to these rules, and one draw needn't show every extreme that they name: Clips are consecutive runs of frames: clip_start never falls, clip_start[t] <= t, clip_start[t] == t at each clip's first frame; every clip has 9 to 33 frames except the last two, which are cut by the bin's end; the bin's last frame begins a clip of its own.
All inputs are finite; a program needn't handle non-finite values.
Results may differ from the reference program's by a relative error of at most 0.012.
Values may be sent and summed in bfloat16 or wider, within the bound.
A program may use at most 128 MiB of HBM per device.

```python
import jax
import jax.numpy as jnp
from jax import lax

C = 512
CL = 16
D = 3072
PATCH_EDGE = 4
TAPS = 3
CLIP_MIN = 9
CLIP_MAX = 33
PIX = 2048
FRAMES = 32
TOKENS = 16384
N_TM = 8
N_SEQ = 4


def draw_clip_start(key, part):
    clip_count = FRAMES // CLIP_MIN + 1
    lengths = jax.random.randint(jax.random.fold_in(key, 17), (clip_count,), CLIP_MIN, CLIP_MAX + 1).astype(jnp.int32)
    clip_ends = jnp.cumsum(lengths).astype(jnp.int32)
    clip_first = clip_ends - lengths
    frame_order = jnp.arange(FRAMES, dtype=jnp.int32)
    owner_clip = jnp.sum((clip_ends[None, :] <= frame_order[:, None]).astype(jnp.int32), axis=1)
    clip_index = jnp.arange(clip_count, dtype=jnp.int32)
    picked = jnp.where(clip_index[None, :] == owner_clip[:, None], clip_first[None, :], 0)
    starts = jnp.sum(picked, axis=1).astype(jnp.int32)
    return jnp.where(frame_order == FRAMES - 1, frame_order, starts).astype(jnp.int32)


def strengthened(drawn, rng, source, target, shards_of, factor):
    owner, partner = [(jnp.arange(drawn.shape[dim]) // (drawn.shape[dim] // shards_of)).reshape([-1 if axis == dim else 1 for axis in range(drawn.ndim)]) for dim in (source, target)]
    chosen = jax.random.permutation(rng, shards_of)[partner]
    strong = (owner == chosen) | (owner == (partner + shards_of // 2) % shards_of)
    return jnp.where(strong, factor * drawn, drawn)


def shard_levels(own_key, extent, split, low, high):
    level = 1.0
    for dim, shards_of in split:
        heights = jax.random.uniform(jax.random.fold_in(jax.random.fold_in(own_key, 6), dim), (shards_of,), jnp.float32, low / len(split), high / len(split))
        level = level * jnp.repeat(jnp.exp(heights), extent[dim] // shards_of).reshape((-1,) + (1,) * (len(extent) - 1 - dim))
    return level


def scatter_about(own_key, shape, width, reach, pieces=(), held_as=jnp.bfloat16):
    values = jax.random.normal(own_key, shape, jnp.float32) * width
    if len(pieces) > 0:
        values = shard_levels(own_key, shape, pieces, -0.22, 0.18) * values
    return jnp.clip(values, min=-reach, max=reach).astype(held_as)


def noise_with(stream_key, dims, scale, most, pieces, heavy, kind=jnp.bfloat16):
    values = scale * jax.random.normal(stream_key, dims, jnp.float32)
    if pieces:
        values = values * shard_levels(stream_key, dims, pieces, -0.22, 0.18)
    return jnp.clip(strengthened(values, jax.random.fold_in(stream_key, 3), *heavy), -most, most).astype(kind)


def setup_inputs(seed: int = 0) -> dict:
    keys = jax.random.split(jax.random.key(seed), 10)
    latents = scatter_about(keys[0], (FRAMES, CL, PIX), 1.0, 6.0, ((0, 8), (2, 4)))
    hidden = scatter_about(keys[1], (TOKENS, D), 1.0, 6.0, ((0, 32),))
    grad_out = noise_with(keys[2], (FRAMES, C, PIX), 1.0, 6.0, ((0, 8), (2, 4)), (0, 1, 8, 2.0))
    conv_in_w = scatter_about(keys[3], (TAPS, C, CL), (TAPS * CL) ** -0.5, 0.875)
    conv_in_b = scatter_about(keys[4], (C,), 1.0, 4.0, (), jnp.float32)
    conv_w = scatter_about(keys[5], (TAPS, C, C), (TAPS * C) ** -0.5, 0.15625)
    final_w = scatter_about(keys[6], (D, CL * PATCH_EDGE), D ** -0.5, 0.109375)
    modulation = scatter_about(keys[7], (2, D), 0.5, 3.0, (), jnp.float32)
    clip_start = draw_clip_start(jax.random.fold_in(keys[9], 71), 0)
    return dict(latents=latents, hidden=hidden, grad_out=grad_out, conv_in_w=conv_in_w, conv_in_b=conv_in_b, conv_w=conv_w, final_w=final_w, modulation=modulation, clip_start=clip_start)


def silu_parts(pre_act):
    sigmoid_v = jax.nn.sigmoid(pre_act)
    return (pre_act * sigmoid_v, sigmoid_v * (1.0 + pre_act * (1.0 - sigmoid_v)))

def reference(latents, hidden, grad_out, conv_in_w, conv_in_b, conv_w, final_w, modulation, clip_start):
    frames = latents.shape[0]
    chans = grad_out.shape[1]
    latent_channels = latents.shape[1]
    frame_order = jnp.arange(frames, dtype=jnp.int32)
    source = [jnp.maximum(frame_order - offset, clip_start).astype(jnp.int32) for offset in range(TAPS)]
    blocks = N_SEQ
    block_width = PIX // blocks

    def to_blocks(array):
        return array.reshape(array.shape[0], array.shape[1], blocks, block_width).transpose(2, 0, 1, 3)
    w_in = conv_in_w.astype(jnp.float32)
    w_mid = conv_w.astype(jnp.float32)

    def decode_block(running_totals, piece_list):
        lat_block, grad_block = piece_list
        lat_f = lat_block.astype(jnp.float32)
        grad_f = grad_block.astype(jnp.float32)
        pre_act = conv_in_b[None, :, None] + sum((jnp.einsum('oc,tcp->top', w_in[offset], lat_f[source[offset]]) for offset in range(TAPS)))
        activation, silu_slope = silu_parts(pre_act)
        act_low = lax.optimization_barrier(activation.astype(jnp.bfloat16))
        act_f = act_low.astype(jnp.float32)
        grad_act = sum((jnp.zeros((frames, chans, block_width), jnp.float32).at[source[offset]].add(jnp.einsum('oi,top->tip', w_mid[offset], grad_f)) for offset in range(TAPS)))
        grad_pre = lax.optimization_barrier((grad_act * silu_slope).astype(jnp.bfloat16))
        pre_f = grad_pre.astype(jnp.float32)
        lat_grad = sum((jnp.zeros((frames, latent_channels, block_width), jnp.float32).at[source[offset]].add(jnp.einsum('oc,top->tcp', w_in[offset], pre_f)) for offset in range(TAPS)))
        conv_term = jnp.stack([jnp.einsum('top,tip->oi', grad_f, act_f[source[offset]]) for offset in range(TAPS)], axis=1)
        in_term = jnp.stack([jnp.einsum('top,tcp->oc', pre_f, lat_f[source[offset]]) for offset in range(TAPS)], axis=0)
        bias_term = lax.optimization_barrier(jnp.sum(pre_f, axis=(0, 2)))
        new_totals = (running_totals[0] + conv_term, running_totals[1] + in_term, running_totals[2] + bias_term)
        return (new_totals, lat_grad.astype(jnp.bfloat16))
    start_totals = (jnp.zeros((chans, TAPS, chans), jnp.float32), jnp.zeros((TAPS, chans, latent_channels), jnp.float32), jnp.zeros((chans,), jnp.float32))
    running_totals, grad_blocks = lax.scan(decode_block, start_totals, (to_blocks(latents), to_blocks(grad_out)))
    convolution_weight_gradient, input_convolution_gradient, input_bias_gradient = running_totals
    latent_grad = grad_blocks.transpose(1, 2, 0, 3).reshape(frames, latent_channels, PIX)
    token_gradient = latent_grad.reshape(frames, latent_channels, PIX // PATCH_EDGE, PATCH_EDGE).transpose(0, 2, 1, 3).reshape(frames * (PIX // PATCH_EDGE), latent_channels * PATCH_EDGE)
    group_list = N_TM * N_SEQ
    rows_per_block = hidden.shape[0] // group_list
    shift_vec = modulation[0]
    scale_vec = modulation[1]

    def transformer_block(running_totals, piece_list):
        hid_block, grad_block = piece_list
        hid_f = hid_block.astype(jnp.float32)
        center = hid_f - lax.optimization_barrier(jnp.mean(hid_f, axis=1, keepdims=True))
        variance = lax.optimization_barrier(jnp.mean(center * center, axis=1, keepdims=True))
        inv_std = lax.rsqrt(variance + 1e-06)
        normed = center * inv_std
        modulated = (normed * (1.0 + scale_vec) + shift_vec).astype(jnp.bfloat16)
        final_term = jnp.dot(modulated.T, grad_block, preferred_element_type=jnp.float32)
        mod_in = jnp.dot(grad_block, final_w.T, preferred_element_type=jnp.float32)
        mod_term = jnp.stack([lax.optimization_barrier(jnp.sum(mod_in, axis=0)), lax.optimization_barrier(jnp.sum(mod_in * normed, axis=0))])
        norm_grad = mod_in * (1.0 + scale_vec)
        hid_grad = inv_std * (norm_grad - lax.optimization_barrier(jnp.mean(norm_grad, axis=1, keepdims=True)) - normed * lax.optimization_barrier(jnp.mean(norm_grad * normed, axis=1, keepdims=True)))
        return ((running_totals[0] + final_term, running_totals[1] + mod_term), hid_grad.astype(jnp.bfloat16))
    transformer_start = (jnp.zeros((hidden.shape[1], latent_channels * PATCH_EDGE), jnp.float32), jnp.zeros((2, hidden.shape[1]), jnp.float32))
    transformer_totals, hidden_blocks = lax.scan(transformer_block, transformer_start, (hidden.reshape(group_list, rows_per_block, hidden.shape[1]), token_gradient.reshape(group_list, rows_per_block, latent_channels * PATCH_EDGE)))
    hidden_input_gradient = hidden_blocks.reshape(hidden.shape[0], hidden.shape[1])
    return (hidden_input_gradient, convolution_weight_gradient, input_convolution_gradient, input_bias_gradient, transformer_totals[0], transformer_totals[1])
```

```python
import functools

import jax
import jax.numpy as jnp
from jax import lax
from jax.experimental import pallas as pl
from jax.experimental.pallas import tpu as pltpu
from jax.sharding import PartitionSpec as P

F32 = jnp.float32
BF16 = jnp.bfloat16
MESH = pl.DeviceIdType.MESH
PATCH = 4
MAX_VMEM = 60 * 1024 * 1024


def dot(a, b, ca, cb):
    return lax.dot_general(a, b, (((ca,), (cb,)), ((), ())), preferred_element_type=F32)


def load_in_weights(w_in_ref, b_ref, w64):
    bias = b_ref[...]
    hi = bias.astype(BF16)
    mid = (bias - hi.astype(F32)).astype(BF16)
    lo = (bias - hi.astype(F32) - mid.astype(F32)).astype(BF16)
    pad = jnp.zeros((16 - 3, bias.shape[1]), F32)
    rows = jnp.concatenate(
        [w_in_ref[...].astype(F32), hi.astype(F32), mid.astype(F32), lo.astype(F32), pad], axis=0
    )
    w64[...] = rows.T.astype(BF16)


def load_window(prev_ref, lat_ref, latx):
    latx[: prev_ref.shape[0]] = prev_ref[...]
    latx[prev_ref.shape[0] :] = lat_ref[...]


def source(clip_ref, frame, tap):
    frames = clip_ref.shape[0]
    return jnp.maximum(frame - tap, clip_ref[jnp.clip(frame, 0, frames - 1)])


def pre_of(clip_ref, latx, z, w64, frame, base):
    cl = latx.shape[1]
    top = latx.shape[0] - 1
    for tap in range(3):
        row = jnp.clip(source(clip_ref, frame, tap) - base, 0, top)
        z[tap * cl : (tap + 1) * cl] = latx[row]
    z[3 * cl :] = jnp.ones_like(z[3 * cl :])
    return dot(w64[...], z[...], 1, 0)


def sigmoid(x):
    return 0.5 * jnp.tanh(0.5 * x) + 0.5


def weight_kernel(clip_ref, prev_ref, lat_ref, grad_ref, w_in_ref, b_ref, out_ref, latx, z, w64, act, acc):
    step = pl.program_id(0)
    slab = lat_ref.shape[0]
    halo = prev_ref.shape[0]
    chans = grad_ref.shape[1]
    first = lax.axis_index("tm") * slab

    def activate(frame):
        pre = pre_of(clip_ref, latx, z, w64, frame, first - halo)
        act[frame - first + 2] = (pre * sigmoid(pre)).astype(BF16)

    @pl.when(step == 0)
    def _():
        load_in_weights(w_in_ref, b_ref, w64)
        load_window(prev_ref, lat_ref, latx)
        acc[...] = jnp.zeros_like(acc)

    @pl.loop(jnp.where(step == 0, -2, step), step + 1)
    def _(t):
        activate(first + t)

    grad = grad_ref[0]
    for tap in range(3):
        row = source(clip_ref, first + step, tap) - first + 2
        acc[:, tap * chans : (tap + 1) * chans] += dot(grad, act[row], 1, 1)

    @pl.when(step == slab - 1)
    def _():
        n_tm, n_seq, rows, _ = out_ref.shape
        for i in range(n_tm):
            for j in range(n_seq):
                at = (i * n_seq + j) * rows
                out_ref[i, j] = acc[at : at + rows, :].astype(BF16)


def latent_kernel(
    clip_ref, prev_ref, lat_ref, grad_ref, next_ref, w_in_ref, b_ref, w_ref,
    lg_ref, misc_ref, latx, z, w64, wt, gx, sem,
):
    step = pl.program_id(0)
    slab = lat_ref.shape[0]
    halo = prev_ref.shape[0]
    chans = w_ref.shape[1]
    cl = lat_ref.shape[1]
    frames = clip_ref.shape[0]
    first = lax.axis_index("tm") * slab

    @pl.when(step == 0)
    def _():
        own = pltpu.make_async_copy(grad_ref, gx.at[pl.ds(0, slab * chans)], sem.at[0])
        own.start()
        following = pltpu.make_async_copy(next_ref, gx.at[pl.ds(slab * chans, 2 * chans)], sem.at[1])
        following.start()
        load_in_weights(w_in_ref, b_ref, w64)
        load_window(prev_ref, lat_ref, latx)
        for tap in range(3):
            wt[:, tap * chans : (tap + 1) * chans] = w_ref[tap].T
        lg_ref[...] = jnp.zeros_like(lg_ref)
        misc_ref[...] = jnp.zeros_like(misc_ref)
        own.wait()
        following.wait()

    s = first + step
    spare = (slab + 2) * chans

    def start_of(frame):
        return jnp.where(frame < frames, clip_ref[jnp.minimum(frame, frames - 1)], frames)

    a1 = start_of(s + 1) <= s
    a2 = start_of(s + 2) <= s
    b0 = start_of(s) == s
    b1 = start_of(s + 1) == s
    plain = a1 & a2 & jnp.logical_not(b0) & jnp.logical_not(b1)

    @pl.when(jnp.logical_not(plain))
    def _():
        g0 = gx[pl.ds(pl.multiple_of(step * chans, chans), chans)]
        g1 = gx[pl.ds(pl.multiple_of((step + 1) * chans, chans), chans)].astype(F32)
        g2 = gx[pl.ds(pl.multiple_of((step + 2) * chans, chans), chans)].astype(F32)
        gf = g0.astype(F32)
        m = [jnp.where(c, 1.0, 0.0).astype(F32) for c in (a1, a2, b0, b1)]
        gx[spare : spare + chans] = g0
        gx[spare + chans : spare + 2 * chans] = (m[0] * g1 + m[2] * gf).astype(BF16)
        gx[spare + 2 * chans : spare + 3 * chans] = (m[1] * g2 + m[3] * g1 + m[2] * gf).astype(BF16)

    at = pl.multiple_of(jnp.where(plain, step * chans, spare), chans)
    grad_act = dot(wt[...], gx[pl.ds(at, 3 * chans)], 1, 0)
    pre = pre_of(clip_ref, latx, z, w64, s, first - halo)
    sig = sigmoid(pre)
    grad_pre = (grad_act * (sig * (1.0 + pre * (1.0 - sig)))).astype(BF16)
    misc_ref[...] += dot(z[...], grad_pre, 1, 1)
    parts = dot(w_in_ref[...], grad_pre, 1, 0)
    for tap in range(3):
        row = source(clip_ref, s, tap) - first + 2
        lg_ref[row] += parts[tap * cl : (tap + 1) * cl]


def token_kernel(
    n_tm, n_seq,
    lg_ref, hid_ref, fw_ref, modu_ref, w4_ref, misc_ref,
    dx_ref, wg_ref, fin_ref, mod_ref, min_ref,
    tok, tok_halo, facc, macc, wrecv, wsum, wrecv2, f4, frecv, fsum, frecv2, gath,
    s_tok, r_tok, s_halo, r_halo, s_w, r_w, s_w2, r_w2, s_f, r_f, s_f2, r_f2, s_g, r_g, s_g2, r_g2,
):
    i = lax.axis_index("tm")
    j = lax.axis_index("seq")
    tms = [(d, lax.rem(i + d, n_tm)) for d in range(1, n_tm)]
    seqs = [(d, lax.rem(j + d, n_seq)) for d in range(1, n_seq)]
    cl = lg_ref.shape[1]
    width = lg_ref.shape[2]
    d_model = hid_ref.shape[1]
    takes_halo = (i < n_tm - 1) & (j >= n_seq - 2)

    barrier = pltpu.get_barrier_semaphore()
    for _, p in tms:
        pl.semaphore_signal(barrier, inc=1, device_id=(p, j), device_id_type=MESH)
    for _, p in seqs:
        pl.semaphore_signal(barrier, inc=1, device_id=(i, p), device_id_type=MESH)

    @pl.when(j >= n_seq - 2)
    def _():
        for p in range(n_seq):
            pl.semaphore_signal(barrier, inc=1, device_id=(lax.rem(i + 1, n_tm), p), device_id_type=MESH)

    pl.semaphore_wait(barrier, n_tm + n_seq)

    def copy(src, dst, send, recv, to):
        return pltpu.make_async_remote_copy(
            src_ref=src, dst_ref=dst, send_sem=send, recv_sem=recv, device_id=to, device_id_type=MESH
        )

    tok_copies = [
        copy(lg_ref.at[2 + p], tok.at[j], s_tok.at[d - 1], r_tok.at[d - 1], (i, p)) for d, p in seqs
    ]

    def halo_copy(h):
        return copy(lg_ref.at[h], tok_halo.at[j], s_halo.at[h], r_halo.at[j], (i - 1, n_seq - 2 + h))

    for c in tok_copies:
        c.start()

    @pl.when(i > 0)
    def _():
        for h in range(2):
            halo_copy(h).start()

    w_copies = [
        copy(w4_ref.at[p], wrecv.at[d - 1], s_w.at[d - 1], r_w.at[d - 1], (p, j)) for d, p in tms
    ]
    for c in w_copies:
        c.start()

    @pl.when(jnp.logical_not(takes_halo))
    def _():
        tok_halo[...] = jnp.zeros_like(tok_halo)

    n = width // PATCH
    row = lax.broadcasted_iota(jnp.int32, (width, width), 0)
    col = lax.broadcasted_iota(jnp.int32, (width, width), 1)
    spread = jnp.where(row == lax.rem(col, n) * PATCH + lax.div(col, n), 1.0, 0.0).astype(BF16)
    e = cl * PATCH
    row = lax.broadcasted_iota(jnp.int32, (e, e), 0)
    col = lax.broadcasted_iota(jnp.int32, (e, e), 1)
    order = jnp.where(row == lax.rem(col, cl) * PATCH + lax.div(col, cl), 1.0, 0.0).astype(BF16)

    facc[...] = jnp.zeros_like(facc)
    macc[...] = jnp.zeros_like(macc)
    for c in tok_copies:
        c.wait()

    @pl.when(i > 0)
    def _():
        for h in range(2):
            halo_copy(h).wait_send()

    @pl.when(takes_halo)
    def _():
        for p in range(n_seq):
            copy(lg_ref.at[0], tok_halo.at[p], s_halo.at[0], r_halo.at[p], (i, j)).wait_recv()

    tok[j] = lg_ref[2 + j]

    shift = modu_ref[0:1, :]
    scale = 1.0 + modu_ref[1:2, :]

    @pl.loop(0, n_seq)
    def _(r):
        lat = (tok[r] + tok_halo[r]).astype(BF16)
        split = dot(lat, spread, 1, 0)
        stack = jnp.concatenate([split[:, q * n : (q + 1) * n] for q in range(PATCH)], axis=0)
        tg_t = dot(order, stack.astype(BF16), 1, 0)
        tg = tg_t.T.astype(BF16)
        rows = pl.ds(pl.multiple_of(r * n, n), n)
        hid = hid_ref[rows, :].astype(F32)
        center = hid - jnp.mean(hid, axis=1, keepdims=True)
        inv = lax.rsqrt(jnp.mean(center * center, axis=1, keepdims=True) + 1e-06)
        normed = center * inv
        modulated = (normed * scale + shift).astype(BF16)
        facc[...] += dot(tg_t.astype(BF16), modulated, 1, 0)
        mod_in = dot(tg, fw_ref[...], 1, 0)
        macc[0:1] += jnp.sum(mod_in, axis=0, keepdims=True)
        macc[1:2] += jnp.sum(mod_in * normed, axis=0, keepdims=True)
        ng = mod_in * scale
        m1 = jnp.mean(ng, axis=1, keepdims=True)
        m2 = jnp.mean(ng * normed, axis=1, keepdims=True)
        dx_ref[rows, :] = (inv * (ng - m1 - normed * m2)).astype(BF16)

    chans = misc_ref.shape[1]
    wf = d_model // n_tm
    wm = chans // n_tm
    er = e // n_seq
    pieces = d_model // chans
    small = jnp.concatenate(
        [misc_ref[0 : 3 * cl + 1, :]]
        + [macc[b : b + 1, p * chans : (p + 1) * chans] for b in range(2) for p in range(pieces)]
        + [jnp.zeros((e - 3 * cl - 1 - 2 * pieces, chans), F32)],
        axis=0,
    )
    for a in range(n_tm):
        for b in range(n_seq):
            f4[a, b, :, :wf] = facc[b * er : (b + 1) * er, a * wf : (a + 1) * wf].astype(BF16)
            f4[a, b, :, wf : wf + wm] = small[b * er : (b + 1) * er, a * wm : (a + 1) * wm].astype(BF16)
            if wf + wm < f4.shape[3]:
                f4[a, b, :, wf + wm :] = jnp.zeros((er, f4.shape[3] - wf - wm), BF16)
    f_copies = [
        copy(f4.at[p], frecv.at[d - 1], s_f.at[d - 1], r_f.at[d - 1], (p, j)) for d, p in tms
    ]
    for c in f_copies:
        c.start()

    for c in w_copies:
        c.wait()
    for b in range(n_seq):
        total = w4_ref[i, b].astype(F32)
        for k in range(n_tm - 1):
            total = total + wrecv[k, b].astype(F32)
        wsum[b] = total.astype(BF16)
    w2_copies = [
        copy(wsum.at[p], wrecv2.at[d - 1], s_w2.at[d - 1], r_w2.at[d - 1], (i, p)) for d, p in seqs
    ]
    for c in w2_copies:
        c.start()

    for c in f_copies:
        c.wait()
    total = f4[i].astype(F32)
    for k in range(n_tm - 1):
        total = total + frecv[k].astype(F32)
    fsum[...] = total.astype(BF16)
    f2_copies = [
        copy(fsum.at[p], frecv2.at[d - 1], s_f2.at[d - 1], r_f2.at[d - 1], (i, p)) for d, p in seqs
    ]
    for c in f2_copies:
        c.start()

    for c in w2_copies:
        c.wait()
    total = wsum[j].astype(F32)
    for k in range(n_seq - 1):
        total = total + wrecv2[k].astype(F32)
    for tap in range(3):
        wg_ref[tap] = total[:, tap * chans : (tap + 1) * chans]

    for c in f2_copies:
        c.wait()
    total = fsum[j].astype(F32)
    for k in range(n_seq - 1):
        total = total + frecv2[k].astype(F32)
    gath[i, j] = total.astype(BF16)
    g_copies = [
        copy(gath.at[i, j], gath.at[i, j], s_g.at[d - 1], r_g.at[d - 1], (i, p)) for d, p in seqs
    ]
    for c in g_copies:
        c.start()
    for c in g_copies:
        c.wait()
    g2_copies = [
        copy(gath.at[i], gath.at[i], s_g2.at[d - 1], r_g2.at[d - 1], (p, j)) for d, p in tms
    ]
    for c in g2_copies:
        c.start()
    for c in g2_copies:
        c.wait()
    for a in range(n_tm):
        for b in range(n_seq):
            fin_ref[b * er : (b + 1) * er, a * wf : (a + 1) * wf] = gath[a, b, :, :wf].astype(F32)
            min_ref[b * er : (b + 1) * er, a * wm : (a + 1) * wm] = gath[a, b, :, wf : wf + wm].astype(F32)
    for b in range(2):
        for p in range(pieces):
            at = 3 * cl + 1 + b * pieces + p
            mod_ref[b : b + 1, p * chans : (p + 1) * chans] = min_ref[at : at + 1, :]


def local(n_tm, n_seq, latents, hidden, grad_out, conv_in_w, conv_in_b, conv_w, final_w, modulation, clip_start):
    slab, cl, width = latents.shape
    taps, chans = conv_w.shape[:2]
    tokens, d_model = hidden.shape
    rows = chans // (n_tm * n_seq)
    backward = [(k, k - 1) for k in range(1, n_tm)]
    forward = [(k, k + 1) for k in range(n_tm - 1)]
    lat_prev = lax.ppermute(latents[slab - 4 :], "tm", forward)
    grad_next = lax.ppermute(grad_out[:2], "tm", backward)
    w_in = conv_in_w.transpose(0, 2, 1).reshape(taps * cl, chans)
    bias = conv_in_b.reshape(1, chans)

    def whole(*shape):
        return pl.BlockSpec(shape, lambda t, c: (0,) * len(shape))

    window = [
        pltpu.VMEM((slab + 4, cl, width), BF16),
        pltpu.VMEM((4 * cl, width), BF16),
        pltpu.VMEM((chans, 4 * cl), BF16),
    ]
    w4 = pl.pallas_call(
        weight_kernel,
        out_shape=jax.ShapeDtypeStruct((n_tm, n_seq, rows, taps * chans), BF16),
        grid_spec=pltpu.PrefetchScalarGridSpec(
            num_scalar_prefetch=1,
            grid=(slab,),
            in_specs=[
                whole(4, cl, width),
                whole(slab, cl, width),
                pl.BlockSpec((1, chans, width), lambda t, c: (t, 0, 0)),
                whole(taps * cl, chans),
                whole(1, chans),
            ],
            out_specs=whole(n_tm, n_seq, rows, taps * chans),
            scratch_shapes=window
            + [pltpu.VMEM((slab + 2, chans, width), BF16), pltpu.VMEM((chans, taps * chans), F32)],
        ),
        compiler_params=pltpu.CompilerParams(vmem_limit_bytes=MAX_VMEM),
        cost_estimate=pl.CostEstimate(flops=7 * 10**9, bytes_accessed=6 * 10**6, transcendentals=2 * 10**6),
        name="weight_grad",
    )(clip_start, lat_prev, latents, grad_out, w_in, bias)

    lg, misc = pl.pallas_call(
        latent_kernel,
        out_shape=(
            jax.ShapeDtypeStruct((slab + 2, cl, width), F32),
            jax.ShapeDtypeStruct((4 * cl, chans), F32),
        ),
        grid_spec=pltpu.PrefetchScalarGridSpec(
            num_scalar_prefetch=1,
            grid=(slab,),
            in_specs=[
                whole(4, cl, width),
                whole(slab, cl, width),
                pl.BlockSpec(memory_space=pl.ANY),
                pl.BlockSpec(memory_space=pl.ANY),
                whole(taps * cl, chans),
                whole(1, chans),
                whole(taps, chans, chans),
            ],
            out_specs=(whole(slab + 2, cl, width), whole(4 * cl, chans)),
            scratch_shapes=window
            + [
                pltpu.VMEM((chans, taps * chans), BF16),
                pltpu.VMEM(((slab + 5) * chans, width), BF16),
                pltpu.SemaphoreType.DMA((2,)),
            ],
        ),
        compiler_params=pltpu.CompilerParams(vmem_limit_bytes=MAX_VMEM),
        cost_estimate=pl.CostEstimate(flops=7 * 10**9, bytes_accessed=6 * 10**6, transcendentals=10**6),
        name="latent_grad",
    )(
        clip_start, lat_prev, latents, grad_out.reshape(slab * chans, width),
        grad_next.reshape(2 * chans, width), w_in, bias, conv_w,
    )

    e = cl * PATCH
    er = e // n_seq
    cw = -(-((d_model + chans) // n_tm) // 128) * 128
    vmem = pl.BlockSpec(memory_space=pltpu.VMEM)
    dma = pltpu.SemaphoreType.DMA
    nt, ns = n_tm - 1, n_seq - 1
    dx, wg, fin, mod, small = pl.pallas_call(
        functools.partial(token_kernel, n_tm, n_seq),
        out_shape=(
            jax.ShapeDtypeStruct((tokens, d_model), BF16),
            jax.ShapeDtypeStruct((taps, rows, chans), F32),
            jax.ShapeDtypeStruct((e, d_model), F32),
            jax.ShapeDtypeStruct((2, d_model), F32),
            jax.ShapeDtypeStruct((e, chans), F32),
        ),
        in_specs=[vmem] * 6,
        out_specs=(vmem,) * 5,
        scratch_shapes=[
            pltpu.VMEM((n_seq, cl, width), F32),
            pltpu.VMEM((n_seq, cl, width), F32),
            pltpu.VMEM((e, d_model), F32),
            pltpu.VMEM((8, d_model), F32),
            pltpu.VMEM((nt, n_seq, rows, taps * chans), BF16),
            pltpu.VMEM((n_seq, rows, taps * chans), BF16),
            pltpu.VMEM((ns, rows, taps * chans), BF16),
            pltpu.VMEM((n_tm, n_seq, er, cw), BF16),
            pltpu.VMEM((nt, n_seq, er, cw), BF16),
            pltpu.VMEM((n_seq, er, cw), BF16),
            pltpu.VMEM((ns, er, cw), BF16),
            pltpu.VMEM((n_tm, n_seq, er, cw), BF16),
            dma((ns,)), dma((ns,)), dma((2,)), dma((n_seq,)),
            dma((nt,)), dma((nt,)), dma((ns,)), dma((ns,)),
            dma((nt,)), dma((nt,)), dma((ns,)), dma((ns,)),
            dma((ns,)), dma((ns,)), dma((nt,)), dma((nt,)),
        ],
        compiler_params=pltpu.CompilerParams(
            vmem_limit_bytes=MAX_VMEM, collective_id=0, has_side_effects=True
        ),
        name="token_grad",
    )(lg, hidden, final_w.T, modulation, w4, misc)
    return (
        dx,
        wg.transpose(1, 0, 2),
        small[: taps * cl].reshape(taps, cl, chans).transpose(0, 2, 1),
        small[taps * cl],
        fin.T,
        mod,
    )


def solution(mesh):
    return jax.shard_map(
        functools.partial(local, mesh.shape["tm"], mesh.shape["seq"]),
        mesh=mesh,
        in_specs=(
            P("tm", None, "seq"),
            P(("tm", "seq"), None),
            P("tm", None, "seq"),
            P(),
            P(),
            P(),
            P(),
            P(),
            P(),
        ),
        out_specs=(P(("tm", "seq"), None), P(("tm", "seq"), None, None), P(), P(), P(), P()),
        check_vma=False,
    )
```

```python
import functools

import jax
import jax.numpy as jnp
from jax import lax
from jax.experimental import pallas as pl
from jax.experimental.pallas import tpu as pltpu
from jax.sharding import PartitionSpec as P

F32 = jnp.float32
BF16 = jnp.bfloat16
MESH = pl.DeviceIdType.MESH
PATCH = 4
MAX_VMEM = 60 * 1024 * 1024


def dot(a, b, ca, cb):
    return lax.dot_general(a, b, (((ca,), (cb,)), ((), ())), preferred_element_type=F32)


def load_in_weights(w_in_ref, b_ref, w64):
    bias = b_ref[...]
    hi = bias.astype(BF16)
    mid = (bias - hi.astype(F32)).astype(BF16)
    lo = (bias - hi.astype(F32) - mid.astype(F32)).astype(BF16)
    pad = jnp.zeros((16 - 3, bias.shape[1]), F32)
    rows = jnp.concatenate(
        [w_in_ref[...].astype(F32), hi.astype(F32), mid.astype(F32), lo.astype(F32), pad], axis=0
    )
    w64[...] = rows.T.astype(BF16)


def load_window(prev_ref, lat_ref, latx):
    latx[: prev_ref.shape[0]] = prev_ref[...]
    latx[prev_ref.shape[0] :] = lat_ref[...]


def source(clip_ref, frame, tap):
    frames = clip_ref.shape[0]
    return jnp.maximum(frame - tap, clip_ref[jnp.clip(frame, 0, frames - 1)])


def pre_of(clip_ref, latx, z, w64, frame, base):
    cl = latx.shape[1]
    top = latx.shape[0] - 1
    for tap in range(3):
        row = jnp.clip(source(clip_ref, frame, tap) - base, 0, top)
        z[tap * cl : (tap + 1) * cl] = latx[row]
    z[3 * cl :] = jnp.ones_like(z[3 * cl :])
    return dot(w64[...], z[...], 1, 0)


def sigmoid(x):
    return 0.5 * jnp.tanh(0.5 * x) + 0.5


def weight_kernel(clip_ref, prev_ref, lat_ref, grad_ref, w_in_ref, b_ref, out_ref, latx, z, w64, act, acc):
    step = pl.program_id(0)
    slab = lat_ref.shape[0]
    halo = prev_ref.shape[0]
    chans = grad_ref.shape[1]
    first = lax.axis_index("tm") * slab

    def activate(frame):
        pre = pre_of(clip_ref, latx, z, w64, frame, first - halo)
        act[frame - first + 2] = (pre * sigmoid(pre)).astype(BF16)

    @pl.when(step == 0)
    def _():
        load_in_weights(w_in_ref, b_ref, w64)
        load_window(prev_ref, lat_ref, latx)
        acc[...] = jnp.zeros_like(acc)

    @pl.loop(jnp.where(step == 0, -2, step), step + 1)
    def _(t):
        activate(first + t)

    grad = grad_ref[0]
    for tap in range(3):
        row = source(clip_ref, first + step, tap) - first + 2
        acc[:, tap * chans : (tap + 1) * chans] += dot(grad, act[row], 1, 1)

    @pl.when(step == slab - 1)
    def _():
        n_tm, n_seq, rows, _ = out_ref.shape
        for i in range(n_tm):
            for j in range(n_seq):
                at = (i * n_seq + j) * rows
                out_ref[i, j] = acc[at : at + rows, :].astype(BF16)


def latent_kernel(
    clip_ref, prev_ref, lat_ref, grad_ref, next_ref, w_in_ref, b_ref, w_ref,
    lg_ref, misc_ref, latx, z, w64, wt, gx, sem,
):
    step = pl.program_id(0)
    slab = lat_ref.shape[0]
    halo = prev_ref.shape[0]
    chans = w_ref.shape[1]
    cl = lat_ref.shape[1]
    frames = clip_ref.shape[0]
    first = lax.axis_index("tm") * slab

    @pl.when(step == 0)
    def _():
        own = pltpu.make_async_copy(grad_ref, gx.at[pl.ds(0, slab * chans)], sem.at[0])
        own.start()
        following = pltpu.make_async_copy(next_ref, gx.at[pl.ds(slab * chans, 2 * chans)], sem.at[1])
        following.start()
        load_in_weights(w_in_ref, b_ref, w64)
        load_window(prev_ref, lat_ref, latx)
        for tap in range(3):
            wt[:, tap * chans : (tap + 1) * chans] = w_ref[tap].T
        lg_ref[...] = jnp.zeros_like(lg_ref)
        misc_ref[...] = jnp.zeros_like(misc_ref)
        own.wait()
        following.wait()

    s = first + step
    spare = (slab + 2) * chans

    def start_of(frame):
        return jnp.where(frame < frames, clip_ref[jnp.minimum(frame, frames - 1)], frames)

    a1 = start_of(s + 1) <= s
    a2 = start_of(s + 2) <= s
    b0 = start_of(s) == s
    b1 = start_of(s + 1) == s
    plain = a1 & a2 & jnp.logical_not(b0) & jnp.logical_not(b1)

    @pl.when(jnp.logical_not(plain))
    def _():
        g0 = gx[pl.ds(pl.multiple_of(step * chans, chans), chans)]
        g1 = gx[pl.ds(pl.multiple_of((step + 1) * chans, chans), chans)].astype(F32)
        g2 = gx[pl.ds(pl.multiple_of((step + 2) * chans, chans), chans)].astype(F32)
        gf = g0.astype(F32)
        m = [jnp.where(c, 1.0, 0.0).astype(F32) for c in (a1, a2, b0, b1)]
        gx[spare : spare + chans] = g0
        gx[spare + chans : spare + 2 * chans] = (m[0] * g1 + m[2] * gf).astype(BF16)
        gx[spare + 2 * chans : spare + 3 * chans] = (m[1] * g2 + m[3] * g1 + m[2] * gf).astype(BF16)

    at = pl.multiple_of(jnp.where(plain, step * chans, spare), chans)
    grad_act = dot(wt[...], gx[pl.ds(at, 3 * chans)], 1, 0)
    pre = pre_of(clip_ref, latx, z, w64, s, first - halo)
    sig = sigmoid(pre)
    grad_pre = (grad_act * (sig * (1.0 + pre * (1.0 - sig)))).astype(BF16)
    misc_ref[...] += dot(z[...], grad_pre, 1, 1)
    parts = dot(w_in_ref[...], grad_pre, 1, 0)
    for tap in range(3):
        row = source(clip_ref, s, tap) - first + 2
        lg_ref[row] += parts[tap * cl : (tap + 1) * cl]


def token_kernel(
    n_tm, n_seq,
    lg_ref, hid_ref, fw_ref, modu_ref, w4_ref, misc_ref,
    dx_ref, wg_ref, gath,
    tok, tok_halo, tgs, tcol, facc, macc, wrecv, wsum, wrecv2, f4, frecv, fsum, frecv2,
    s_tok, r_tok, s_halo, r_halo, s_w, r_w, s_w2, r_w2, s_f, r_f, s_f2, r_f2, s_g, r_g, s_g2, r_g2,
):
    i = lax.axis_index("tm")
    j = lax.axis_index("seq")
    tms = [(d, lax.rem(i + d, n_tm)) for d in range(1, n_tm)]
    seqs = [(d, lax.rem(j + d, n_seq)) for d in range(1, n_seq)]
    cl = lg_ref.shape[1]
    width = lg_ref.shape[2]
    d_model = hid_ref.shape[1]
    takes_halo = (i < n_tm - 1) & (j >= n_seq - 2)

    barrier = pltpu.get_barrier_semaphore()
    for _, p in tms:
        pl.semaphore_signal(barrier, inc=1, device_id=(p, j), device_id_type=MESH)
    for _, p in seqs:
        pl.semaphore_signal(barrier, inc=1, device_id=(i, p), device_id_type=MESH)

    @pl.when(j >= n_seq - 2)
    def _():
        for p in range(n_seq):
            pl.semaphore_signal(barrier, inc=1, device_id=(lax.rem(i + 1, n_tm), p), device_id_type=MESH)

    pl.semaphore_wait(barrier, n_tm + n_seq)

    def copy(src, dst, send, recv, to):
        return pltpu.make_async_remote_copy(
            src_ref=src, dst_ref=dst, send_sem=send, recv_sem=recv, device_id=to, device_id_type=MESH
        )

    tok_copies = [
        copy(lg_ref.at[2 + p], tok.at[j], s_tok.at[d - 1], r_tok.at[d - 1], (i, p)) for d, p in seqs
    ]

    def halo_copy(h):
        return copy(lg_ref.at[h], tok_halo.at[j], s_halo.at[h], r_halo.at[j], (i - 1, n_seq - 2 + h))

    for c in tok_copies:
        c.start()

    @pl.when(i > 0)
    def _():
        for h in range(2):
            halo_copy(h).start()

    w_copies = [
        copy(w4_ref.at[p], wrecv.at[d - 1], s_w.at[d - 1], r_w.at[d - 1], (p, j)) for d, p in tms
    ]
    for c in w_copies:
        c.start()

    @pl.when(jnp.logical_not(takes_halo))
    def _():
        tok_halo[...] = jnp.zeros_like(tok_halo)

    n = width // PATCH
    row = lax.broadcasted_iota(jnp.int32, (width, width), 0)
    col = lax.broadcasted_iota(jnp.int32, (width, width), 1)
    spread = jnp.where(row == lax.rem(col, n) * PATCH + lax.div(col, n), 1.0, 0.0).astype(BF16)
    e = cl * PATCH
    row = lax.broadcasted_iota(jnp.int32, (e, e), 0)
    col = lax.broadcasted_iota(jnp.int32, (e, e), 1)
    order = jnp.where(row == lax.rem(col, cl) * PATCH + lax.div(col, cl), 1.0, 0.0).astype(BF16)

    facc[...] = jnp.zeros_like(facc)
    tcol[...] = jnp.zeros_like(tcol)
    for c in tok_copies:
        c.wait()

    @pl.when(i > 0)
    def _():
        for h in range(2):
            halo_copy(h).wait_send()

    @pl.when(takes_halo)
    def _():
        for p in range(n_seq):
            copy(lg_ref.at[0], tok_halo.at[p], s_halo.at[0], r_halo.at[p], (i, j)).wait_recv()

    tok[j] = lg_ref[2 + j]

    shift = modu_ref[0:1, :]
    scale = 1.0 + modu_ref[1:2, :]

    def rows_of(r):
        return pl.ds(pl.multiple_of(r * n, n), n)

    def normalise(r):
        hid = hid_ref[rows_of(r), :].astype(F32)
        center = hid - jnp.mean(hid, axis=1, keepdims=True)
        inv = lax.rsqrt(jnp.mean(center * center, axis=1, keepdims=True) + 1e-06)
        return center * inv, inv

    @pl.loop(0, n_seq)
    def _(r):
        lat = (tok[r] + tok_halo[r]).astype(BF16)
        split = dot(lat, spread, 1, 0)
        stack = jnp.concatenate([split[:, q * n : (q + 1) * n] for q in range(PATCH)], axis=0)
        tg_t = dot(order, stack.astype(BF16), 1, 0)
        tgs[rows_of(r), :] = tg_t.T.astype(BF16)
        normed, _ = normalise(r)
        facc[...] += dot(tg_t.astype(BF16), normed.astype(BF16), 1, 0)
        tcol[...] += jnp.broadcast_to(jnp.sum(tg_t, axis=1, keepdims=True), tcol.shape)

    column = tcol[:, 0:1]
    fw = fw_ref[...].astype(F32)
    macc[0:1] = jnp.sum(fw * column, axis=0, keepdims=True)
    macc[1:2] = jnp.sum(fw * facc[...], axis=0, keepdims=True)
    facc[...] = facc[...] * scale + column * shift

    chans = misc_ref.shape[1]
    wf = d_model // n_tm
    wm = chans // n_tm
    er = e // n_seq
    pieces = d_model // chans
    small = jnp.concatenate(
        [misc_ref[0 : 3 * cl + 1, :]]
        + [macc[b : b + 1, p * chans : (p + 1) * chans] for b in range(2) for p in range(pieces)]
        + [jnp.zeros((e - 3 * cl - 1 - 2 * pieces, chans), F32)],
        axis=0,
    )
    for a in range(n_tm):
        for b in range(n_seq):
            f4[a, b, :, :wf] = facc[b * er : (b + 1) * er, a * wf : (a + 1) * wf].astype(BF16)
            f4[a, b, :, wf : wf + wm] = small[b * er : (b + 1) * er, a * wm : (a + 1) * wm].astype(BF16)
            if wf + wm < f4.shape[3]:
                f4[a, b, :, wf + wm :] = jnp.zeros((er, f4.shape[3] - wf - wm), BF16)
    f_copies = [
        copy(f4.at[p], frecv.at[d - 1], s_f.at[d - 1], r_f.at[d - 1], (p, j)) for d, p in tms
    ]
    for c in f_copies:
        c.start()

    @pl.loop(0, n_seq)
    def _(r):
        normed, inv = normalise(r)
        ng = dot(tgs[rows_of(r), :], fw_ref[...], 1, 0) * scale
        m1 = jnp.mean(ng, axis=1, keepdims=True)
        m2 = jnp.mean(ng * normed, axis=1, keepdims=True)
        dx_ref[rows_of(r), :] = (inv * (ng - m1 - normed * m2)).astype(BF16)

    for c in w_copies:
        c.wait()
    for b in range(n_seq):
        total = w4_ref[i, b].astype(F32)
        for k in range(n_tm - 1):
            total = total + wrecv[k, b].astype(F32)
        wsum[b] = total.astype(BF16)
    w2_copies = [
        copy(wsum.at[p], wrecv2.at[d - 1], s_w2.at[d - 1], r_w2.at[d - 1], (i, p)) for d, p in seqs
    ]
    for c in w2_copies:
        c.start()

    for c in f_copies:
        c.wait()
    total = f4[i].astype(F32)
    for k in range(n_tm - 1):
        total = total + frecv[k].astype(F32)
    fsum[...] = total.astype(BF16)
    f2_copies = [
        copy(fsum.at[p], frecv2.at[d - 1], s_f2.at[d - 1], r_f2.at[d - 1], (i, p)) for d, p in seqs
    ]
    for c in f2_copies:
        c.start()

    for c in w2_copies:
        c.wait()
    total = wsum[j].astype(F32)
    for k in range(n_seq - 1):
        total = total + wrecv2[k].astype(F32)
    for tap in range(3):
        wg_ref[tap] = total[:, tap * chans : (tap + 1) * chans]

    for c in f2_copies:
        c.wait()
    total = fsum[j].astype(F32)
    for k in range(n_seq - 1):
        total = total + frecv2[k].astype(F32)
    gath[i, j] = total.astype(BF16)
    g_copies = [
        copy(gath.at[i, j], gath.at[i, j], s_g.at[d - 1], r_g.at[d - 1], (i, p)) for d, p in seqs
    ]
    for c in g_copies:
        c.start()
    for c in g_copies:
        c.wait()
    g2_copies = [
        copy(gath.at[i], gath.at[i], s_g2.at[d - 1], r_g2.at[d - 1], (p, j)) for d, p in tms
    ]
    for c in g2_copies:
        c.start()
    for c in g2_copies:
        c.wait()


def unpack_kernel(gath, wg_ref, fin_ref, mod_ref, in_ref, bias_ref, wg_out, small):
    n_tm, n_seq, er, _ = gath.shape
    d_model = fin_ref.shape[1]
    taps_cl, chans = in_ref.shape
    wf = d_model // n_tm
    wm = chans // n_tm
    pieces = d_model // chans
    for a in range(n_tm):
        for b in range(n_seq):
            fin_ref[b * er : (b + 1) * er, a * wf : (a + 1) * wf] = gath[a, b, :, :wf].astype(F32)
            small[b * er : (b + 1) * er, a * wm : (a + 1) * wm] = gath[a, b, :, wf : wf + wm].astype(F32)
    in_ref[...] = small[:taps_cl, :]
    bias_ref[...] = small[taps_cl : taps_cl + 1, :]
    for b in range(2):
        for p in range(pieces):
            at = taps_cl + 1 + b * pieces + p
            mod_ref[b : b + 1, p * chans : (p + 1) * chans] = small[at : at + 1, :]
    wg_out[...] = wg_ref[...]


def local(n_tm, n_seq, latents, hidden, grad_out, conv_in_w, conv_in_b, conv_w, final_w, modulation, clip_start):
    slab, cl, width = latents.shape
    taps, chans = conv_w.shape[:2]
    tokens, d_model = hidden.shape
    rows = chans // (n_tm * n_seq)
    backward = [(k, k - 1) for k in range(1, n_tm)]
    forward = [(k, k + 1) for k in range(n_tm - 1)]
    lat_prev = lax.ppermute(latents[slab - 4 :], "tm", forward)
    grad_next = lax.ppermute(grad_out[:2], "tm", backward)
    w_in = conv_in_w.transpose(0, 2, 1).reshape(taps * cl, chans)
    bias = conv_in_b.reshape(1, chans)

    def whole(*shape):
        return pl.BlockSpec(shape, lambda t, c: (0,) * len(shape))

    window = [
        pltpu.VMEM((slab + 4, cl, width), BF16),
        pltpu.VMEM((4 * cl, width), BF16),
        pltpu.VMEM((chans, 4 * cl), BF16),
    ]
    w4 = pl.pallas_call(
        weight_kernel,
        out_shape=jax.ShapeDtypeStruct((n_tm, n_seq, rows, taps * chans), BF16),
        grid_spec=pltpu.PrefetchScalarGridSpec(
            num_scalar_prefetch=1,
            grid=(slab,),
            in_specs=[
                whole(4, cl, width),
                whole(slab, cl, width),
                pl.BlockSpec((1, chans, width), lambda t, c: (t, 0, 0)),
                whole(taps * cl, chans),
                whole(1, chans),
            ],
            out_specs=whole(n_tm, n_seq, rows, taps * chans),
            scratch_shapes=window
            + [pltpu.VMEM((slab + 2, chans, width), BF16), pltpu.VMEM((chans, taps * chans), F32)],
        ),
        compiler_params=pltpu.CompilerParams(vmem_limit_bytes=MAX_VMEM),
        cost_estimate=pl.CostEstimate(flops=7 * 10**9, bytes_accessed=6 * 10**6, transcendentals=2 * 10**6),
        name="weight_grad",
    )(clip_start, lat_prev, latents, grad_out, w_in, bias)

    lg, misc = pl.pallas_call(
        latent_kernel,
        out_shape=(
            jax.ShapeDtypeStruct((slab + 2, cl, width), F32),
            jax.ShapeDtypeStruct((4 * cl, chans), F32),
        ),
        grid_spec=pltpu.PrefetchScalarGridSpec(
            num_scalar_prefetch=1,
            grid=(slab,),
            in_specs=[
                whole(4, cl, width),
                whole(slab, cl, width),
                pl.BlockSpec(memory_space=pl.ANY),
                pl.BlockSpec(memory_space=pl.ANY),
                whole(taps * cl, chans),
                whole(1, chans),
                whole(taps, chans, chans),
            ],
            out_specs=(whole(slab + 2, cl, width), whole(4 * cl, chans)),
            scratch_shapes=window
            + [
                pltpu.VMEM((chans, taps * chans), BF16),
                pltpu.VMEM(((slab + 5) * chans, width), BF16),
                pltpu.SemaphoreType.DMA((2,)),
            ],
        ),
        compiler_params=pltpu.CompilerParams(vmem_limit_bytes=MAX_VMEM),
        cost_estimate=pl.CostEstimate(flops=7 * 10**9, bytes_accessed=6 * 10**6, transcendentals=10**6),
        name="latent_grad",
    )(
        clip_start, lat_prev, latents, grad_out.reshape(slab * chans, width),
        grad_next.reshape(2 * chans, width), w_in, bias, conv_w,
    )

    e = cl * PATCH
    er = e // n_seq
    cw = -(-((d_model + chans) // n_tm) // 128) * 128
    vmem = pl.BlockSpec(memory_space=pltpu.VMEM)
    dma = pltpu.SemaphoreType.DMA
    nt, ns = n_tm - 1, n_seq - 1
    dx, wg, gath = pl.pallas_call(
        functools.partial(token_kernel, n_tm, n_seq),
        out_shape=(
            jax.ShapeDtypeStruct((tokens, d_model), BF16),
            jax.ShapeDtypeStruct((taps, rows, chans), F32),
            jax.ShapeDtypeStruct((n_tm, n_seq, er, cw), BF16),
        ),
        in_specs=[vmem] * 6,
        out_specs=(vmem,) * 3,
        scratch_shapes=[
            pltpu.VMEM((n_seq, cl, width), F32),
            pltpu.VMEM((n_seq, cl, width), F32),
            pltpu.VMEM((tokens, e), BF16),
            pltpu.VMEM((e, 128), F32),
            pltpu.VMEM((e, d_model), F32),
            pltpu.VMEM((8, d_model), F32),
            pltpu.VMEM((nt, n_seq, rows, taps * chans), BF16),
            pltpu.VMEM((n_seq, rows, taps * chans), BF16),
            pltpu.VMEM((ns, rows, taps * chans), BF16),
            pltpu.VMEM((n_tm, n_seq, er, cw), BF16),
            pltpu.VMEM((nt, n_seq, er, cw), BF16),
            pltpu.VMEM((n_seq, er, cw), BF16),
            pltpu.VMEM((ns, er, cw), BF16),
            dma((ns,)), dma((ns,)), dma((2,)), dma((n_seq,)),
            dma((nt,)), dma((nt,)), dma((ns,)), dma((ns,)),
            dma((nt,)), dma((nt,)), dma((ns,)), dma((ns,)),
            dma((ns,)), dma((ns,)), dma((nt,)), dma((nt,)),
        ],
        compiler_params=pltpu.CompilerParams(
            vmem_limit_bytes=MAX_VMEM, collective_id=0, has_side_effects=True
        ),
        name="token_grad",
    )(lg, hidden, final_w.T, modulation, w4, misc)
    fin, mod, w_in_grad, bias_grad, wg = pl.pallas_call(
        unpack_kernel,
        out_shape=(
            jax.ShapeDtypeStruct((e, d_model), F32),
            jax.ShapeDtypeStruct((2, d_model), F32),
            jax.ShapeDtypeStruct((taps * cl, chans), F32),
            jax.ShapeDtypeStruct((1, chans), F32),
            jax.ShapeDtypeStruct((taps, rows, chans), F32),
        ),
        in_specs=[vmem] * 2,
        out_specs=(vmem,) * 5,
        scratch_shapes=[pltpu.VMEM((e, chans), F32)],
        name="unpack",
    )(gath, wg)
    return (
        dx,
        wg.transpose(1, 0, 2),
        w_in_grad.reshape(taps, cl, chans).transpose(0, 2, 1),
        bias_grad.reshape(chans),
        fin.T,
        mod,
    )


def solution(mesh):
    return jax.shard_map(
        functools.partial(local, mesh.shape["tm"], mesh.shape["seq"]),
        mesh=mesh,
        in_specs=(
            P("tm", None, "seq"),
            P(("tm", "seq"), None),
            P("tm", None, "seq"),
            P(),
            P(),
            P(),
            P(),
            P(),
            P(),
        ),
        out_specs=(P(("tm", "seq"), None), P(("tm", "seq"), None, None), P(), P(), P(), P()),
        check_vma=False,
    )
```

```python
import functools

import jax
import jax.numpy as jnp
from jax import lax
from jax.experimental import pallas as pl
from jax.experimental.pallas import tpu as pltpu
from jax.sharding import PartitionSpec as P

F32 = jnp.float32
BF16 = jnp.bfloat16
MESH = pl.DeviceIdType.MESH
PATCH = 4
CORES = 2
MAX_VMEM = 60 * 1024 * 1024


def dot(a, b, ca, cb):
    return lax.dot_general(a, b, (((ca,), (cb,)), ((), ())), preferred_element_type=F32)


def load_in_weights(w_in_ref, b_ref, w64):
    bias = b_ref[...]
    hi = bias.astype(BF16)
    mid = (bias - hi.astype(F32)).astype(BF16)
    lo = (bias - hi.astype(F32) - mid.astype(F32)).astype(BF16)
    pad = jnp.zeros((16 - 3, bias.shape[1]), F32)
    rows = jnp.concatenate(
        [w_in_ref[...].astype(F32), hi.astype(F32), mid.astype(F32), lo.astype(F32), pad], axis=0
    )
    w64[...] = rows.T.astype(BF16)


def load_window(prev_ref, lat_ref, latx):
    latx[: prev_ref.shape[0]] = prev_ref[...]
    latx[prev_ref.shape[0] :] = lat_ref[...]


def source(clip_ref, frame, tap):
    frames = clip_ref.shape[0]
    return jnp.maximum(frame - tap, clip_ref[jnp.clip(frame, 0, frames - 1)])


def pre_of(clip_ref, latx, z, w64, frame, base):
    cl = latx.shape[1]
    top = latx.shape[0] - 1
    for tap in range(3):
        row = jnp.clip(source(clip_ref, frame, tap) - base, 0, top)
        z[tap * cl : (tap + 1) * cl] = latx[row]
    z[3 * cl :] = jnp.ones_like(z[3 * cl :])
    return dot(w64[...], z[...], 1, 0)


def sigmoid(x):
    return 0.5 * jnp.tanh(0.5 * x) + 0.5


def weight_kernel(clip_ref, prev_ref, lat_ref, grad_ref, w_in_ref, b_ref, out_ref, latx, z, w64, act, acc):
    step = pl.program_id(0)
    slab = lat_ref.shape[0]
    halo = prev_ref.shape[0]
    chans = grad_ref.shape[1]
    first = lax.axis_index("tm") * slab

    def activate(frame):
        pre = pre_of(clip_ref, latx, z, w64, frame, first - halo)
        act[frame - first + 2] = (pre * sigmoid(pre)).astype(BF16)

    @pl.when(step == 0)
    def _():
        load_in_weights(w_in_ref, b_ref, w64)
        load_window(prev_ref, lat_ref, latx)
        acc[...] = jnp.zeros_like(acc)

    @pl.loop(jnp.where(step == 0, -2, step), step + 1)
    def _(t):
        activate(first + t)

    grad = grad_ref[0]
    for tap in range(3):
        row = source(clip_ref, first + step, tap) - first + 2
        acc[:, tap * chans : (tap + 1) * chans] += dot(grad, act[row], 1, 1)

    @pl.when(step == slab - 1)
    def _():
        cores, chips, n_seq, rows, _ = out_ref.shape
        for i in range(cores * chips):
            for j in range(n_seq):
                at = (i * n_seq + j) * rows
                out_ref[i % cores, i // cores, j] = acc[at : at + rows, :].astype(BF16)


def latent_kernel(
    clip_ref, prev_ref, lat_ref, grad_ref, next_ref, w_in_ref, b_ref, w_ref,
    lg_ref, misc_ref, latx, z, w64, wt, gx, sem,
):
    step = pl.program_id(0)
    slab = lat_ref.shape[0]
    halo = prev_ref.shape[0]
    chans = w_ref.shape[1]
    cl = lat_ref.shape[1]
    frames = clip_ref.shape[0]
    first = lax.axis_index("tm") * slab

    @pl.when(step == 0)
    def _():
        own = pltpu.make_async_copy(grad_ref, gx.at[pl.ds(0, slab * chans)], sem.at[0])
        own.start()
        following = pltpu.make_async_copy(next_ref, gx.at[pl.ds(slab * chans, 2 * chans)], sem.at[1])
        following.start()
        load_in_weights(w_in_ref, b_ref, w64)
        load_window(prev_ref, lat_ref, latx)
        for tap in range(3):
            wt[:, tap * chans : (tap + 1) * chans] = w_ref[tap].T
        lg_ref[...] = jnp.zeros_like(lg_ref)
        misc_ref[...] = jnp.zeros_like(misc_ref)
        own.wait()
        following.wait()

    s = first + step
    spare = (slab + 2) * chans

    def start_of(frame):
        return jnp.where(frame < frames, clip_ref[jnp.minimum(frame, frames - 1)], frames)

    a1 = start_of(s + 1) <= s
    a2 = start_of(s + 2) <= s
    b0 = start_of(s) == s
    b1 = start_of(s + 1) == s
    plain = a1 & a2 & jnp.logical_not(b0) & jnp.logical_not(b1)

    @pl.when(jnp.logical_not(plain))
    def _():
        g0 = gx[pl.ds(pl.multiple_of(step * chans, chans), chans)]
        g1 = gx[pl.ds(pl.multiple_of((step + 1) * chans, chans), chans)].astype(F32)
        g2 = gx[pl.ds(pl.multiple_of((step + 2) * chans, chans), chans)].astype(F32)
        gf = g0.astype(F32)
        m = [jnp.where(c, 1.0, 0.0).astype(F32) for c in (a1, a2, b0, b1)]
        gx[spare : spare + chans] = g0
        gx[spare + chans : spare + 2 * chans] = (m[0] * g1 + m[2] * gf).astype(BF16)
        gx[spare + 2 * chans : spare + 3 * chans] = (m[1] * g2 + m[3] * g1 + m[2] * gf).astype(BF16)

    at = pl.multiple_of(jnp.where(plain, step * chans, spare), chans)
    grad_act = dot(wt[...], gx[pl.ds(at, 3 * chans)], 1, 0)
    pre = pre_of(clip_ref, latx, z, w64, s, first - halo)
    sig = sigmoid(pre)
    grad_pre = (grad_act * (sig * (1.0 + pre * (1.0 - sig)))).astype(BF16)
    misc_ref[...] += dot(z[...], grad_pre, 1, 1)
    parts = dot(w_in_ref[...], grad_pre, 1, 0)
    for tap in range(3):
        row = source(clip_ref, s, tap) - first + 2
        lg_ref[row] += parts[tap * cl : (tap + 1) * cl]


def token_kernel(
    n_tm, n_seq,
    lg_ref, hid_ref, fw_ref, modu_ref, w4_ref, misc_ref,
    dx_ref, wg_ref, gath,
    tok, tok_halo, tgs, tcol, facc, macc, wcore, whalf, wrecv, wsum, wrecv2, f4, fcore, fhalf, frecv, fsum, frecv2,
    s_tok, r_tok, s_halo, r_halo, s_w, r_w, s_w2, r_w2, s_f, r_f, s_f2, r_f2, s_g, r_g, s_g2, r_g2, s_core, r_core,
):
    i = lax.axis_index("tm")
    j = lax.axis_index("seq")
    chips = n_tm // CORES
    core = lax.rem(i, CORES)
    chip = lax.div(i, CORES)
    other = CORES - 1 - core
    sibling = (chip * CORES + other, j)
    tms = [(d, lax.rem(chip + d, chips)) for d in range(1, chips)]
    seqs = [(d, lax.rem(j + d, n_seq)) for d in range(1, n_seq)]
    cl = lg_ref.shape[1]
    width = lg_ref.shape[2]
    d_model = hid_ref.shape[1]
    takes_halo = (i < n_tm - 1) & (j >= n_seq - 2)

    barrier = pltpu.get_barrier_semaphore()
    for _, p in tms:
        pl.semaphore_signal(barrier, inc=1, device_id=(p * CORES + core, j), device_id_type=MESH)
    pl.semaphore_signal(barrier, inc=1, device_id=sibling, device_id_type=MESH)
    for _, p in seqs:
        pl.semaphore_signal(barrier, inc=1, device_id=(i, p), device_id_type=MESH)

    @pl.when(j >= n_seq - 2)
    def _():
        for p in range(n_seq):
            pl.semaphore_signal(barrier, inc=1, device_id=(lax.rem(i + 1, n_tm), p), device_id_type=MESH)

    pl.semaphore_wait(barrier, chips + n_seq + 1)

    def copy(src, dst, send, recv, to):
        return pltpu.make_async_remote_copy(
            src_ref=src, dst_ref=dst, send_sem=send, recv_sem=recv, device_id=to, device_id_type=MESH
        )

    tok_copies = [
        copy(lg_ref.at[2 + p], tok.at[j], s_tok.at[d - 1], r_tok.at[d - 1], (i, p)) for d, p in seqs
    ]

    def halo_copy(h):
        return copy(lg_ref.at[h], tok_halo.at[j], s_halo.at[h], r_halo.at[j], (i - 1, n_seq - 2 + h))

    for c in tok_copies:
        c.start()

    @pl.when(i > 0)
    def _():
        for h in range(2):
            halo_copy(h).start()

    w_core = copy(w4_ref.at[other], wcore, s_core.at[0], r_core.at[0], sibling)
    w_core.start()

    @pl.when(jnp.logical_not(takes_halo))
    def _():
        tok_halo[...] = jnp.zeros_like(tok_halo)

    n = width // PATCH
    row = lax.broadcasted_iota(jnp.int32, (width, width), 0)
    col = lax.broadcasted_iota(jnp.int32, (width, width), 1)
    spread = jnp.where(row == lax.rem(col, n) * PATCH + lax.div(col, n), 1.0, 0.0).astype(BF16)
    e = cl * PATCH
    row = lax.broadcasted_iota(jnp.int32, (e, e), 0)
    col = lax.broadcasted_iota(jnp.int32, (e, e), 1)
    order = jnp.where(row == lax.rem(col, cl) * PATCH + lax.div(col, cl), 1.0, 0.0).astype(BF16)

    facc[...] = jnp.zeros_like(facc)
    tcol[...] = jnp.zeros_like(tcol)
    w_core.wait()
    for q in range(chips):
        whalf[q] = (w4_ref[core, q].astype(F32) + wcore[q].astype(F32)).astype(BF16)
    w_copies = [
        copy(whalf.at[p], wrecv.at[d - 1], s_w.at[d - 1], r_w.at[d - 1], (p * CORES + core, j))
        for d, p in tms
    ]
    for c in w_copies:
        c.start()
    for c in tok_copies:
        c.wait()

    @pl.when(i > 0)
    def _():
        for h in range(2):
            halo_copy(h).wait_send()

    @pl.when(takes_halo)
    def _():
        for p in range(n_seq):
            copy(lg_ref.at[0], tok_halo.at[p], s_halo.at[0], r_halo.at[p], (i, j)).wait_recv()

    tok[j] = lg_ref[2 + j]

    shift = modu_ref[0:1, :]
    scale = 1.0 + modu_ref[1:2, :]

    def rows_of(r):
        return pl.ds(pl.multiple_of(r * n, n), n)

    def normalise(r):
        hid = hid_ref[rows_of(r), :].astype(F32)
        center = hid - jnp.mean(hid, axis=1, keepdims=True)
        inv = lax.rsqrt(jnp.mean(center * center, axis=1, keepdims=True) + 1e-06)
        return center * inv, inv

    @pl.loop(0, n_seq)
    def _(r):
        lat = (tok[r] + tok_halo[r]).astype(BF16)
        split = dot(lat, spread, 1, 0)
        stack = jnp.concatenate([split[:, q * n : (q + 1) * n] for q in range(PATCH)], axis=0)
        tg_t = dot(order, stack.astype(BF16), 1, 0)
        tgs[rows_of(r), :] = tg_t.T.astype(BF16)
        normed, _ = normalise(r)
        facc[...] += dot(tg_t.astype(BF16), normed.astype(BF16), 1, 0)
        tcol[...] += jnp.broadcast_to(jnp.sum(tg_t, axis=1, keepdims=True), tcol.shape)

    column = tcol[:, 0:1]
    fw = fw_ref[...].astype(F32)
    macc[0:1] = jnp.sum(fw * column, axis=0, keepdims=True)
    macc[1:2] = jnp.sum(fw * facc[...], axis=0, keepdims=True)
    facc[...] = facc[...] * scale + column * shift

    chans = misc_ref.shape[1]
    wf = d_model // n_tm
    wm = chans // n_tm
    er = e // n_seq
    pieces = d_model // chans
    small = jnp.concatenate(
        [misc_ref[0 : 3 * cl + 1, :]]
        + [macc[b : b + 1, p * chans : (p + 1) * chans] for b in range(2) for p in range(pieces)]
        + [jnp.zeros((e - 3 * cl - 1 - 2 * pieces, chans), F32)],
        axis=0,
    )
    for a in range(n_tm):
        for b in range(n_seq):
            f4[a % CORES, a // CORES, b, :, :wf] = facc[b * er : (b + 1) * er, a * wf : (a + 1) * wf].astype(BF16)
            f4[a % CORES, a // CORES, b, :, wf : wf + wm] = small[b * er : (b + 1) * er, a * wm : (a + 1) * wm].astype(BF16)
            if wf + wm < f4.shape[4]:
                f4[a % CORES, a // CORES, b, :, wf + wm :] = jnp.zeros((er, f4.shape[4] - wf - wm), BF16)
    f_core = copy(f4.at[other], fcore, s_core.at[1], r_core.at[1], sibling)
    f_core.start()

    def input_gradient(r):
        normed, inv = normalise(r)
        ng = dot(tgs[rows_of(r), :], fw_ref[...], 1, 0) * scale
        m1 = jnp.mean(ng, axis=1, keepdims=True)
        m2 = jnp.mean(ng * normed, axis=1, keepdims=True)
        dx_ref[rows_of(r), :] = (inv * (ng - m1 - normed * m2)).astype(BF16)

    pl.loop(0, n_seq // 2)(input_gradient)
    f_core.wait()
    for q in range(chips):
        fhalf[q] = (f4[core, q].astype(F32) + fcore[q].astype(F32)).astype(BF16)
    f_copies = [
        copy(fhalf.at[p], frecv.at[d - 1], s_f.at[d - 1], r_f.at[d - 1], (p * CORES + core, j))
        for d, p in tms
    ]
    for c in f_copies:
        c.start()
    pl.loop(n_seq // 2, n_seq)(input_gradient)

    for c in w_copies:
        c.wait()
    for b in range(n_seq):
        total = whalf[chip, b].astype(F32)
        for k in range(chips - 1):
            total = total + wrecv[k, b].astype(F32)
        wsum[b] = total.astype(BF16)
    w2_copies = [
        copy(wsum.at[p], wrecv2.at[d - 1], s_w2.at[d - 1], r_w2.at[d - 1], (i, p)) for d, p in seqs
    ]
    for c in w2_copies:
        c.start()

    for c in f_copies:
        c.wait()
    total = fhalf[chip].astype(F32)
    for k in range(chips - 1):
        total = total + frecv[k].astype(F32)
    fsum[...] = total.astype(BF16)
    f2_copies = [
        copy(fsum.at[p], frecv2.at[d - 1], s_f2.at[d - 1], r_f2.at[d - 1], (i, p)) for d, p in seqs
    ]
    for c in f2_copies:
        c.start()

    for c in w2_copies:
        c.wait()
    total = wsum[j].astype(F32)
    for k in range(n_seq - 1):
        total = total + wrecv2[k].astype(F32)
    for tap in range(3):
        wg_ref[tap] = total[:, tap * chans : (tap + 1) * chans]

    for c in f2_copies:
        c.wait()
    total = fsum[j].astype(F32)
    for k in range(n_seq - 1):
        total = total + frecv2[k].astype(F32)
    gath[core, chip, j] = total.astype(BF16)
    g_copies = [
        copy(gath.at[core, chip, j], gath.at[core, chip, j], s_g.at[d - 1], r_g.at[d - 1], (i, p)) for d, p in seqs
    ]
    for c in g_copies:
        c.start()
    for c in g_copies:
        c.wait()
    g2_copies = [
        copy(gath.at[core, chip], gath.at[core, chip], s_g2.at[d - 1], r_g2.at[d - 1], (p * CORES + core, j))
        for d, p in tms
    ]
    for c in g2_copies:
        c.start()
    for c in g2_copies:
        c.wait()
    g_core = copy(gath.at[core], gath.at[core], s_core.at[2], r_core.at[2], sibling)
    g_core.start()
    g_core.wait()


def unpack_kernel(gath, wg_ref, fin_ref, mod_ref, in_ref, bias_ref, wg_out, small):
    cores, chips, n_seq, er, _ = gath.shape
    n_tm = cores * chips
    d_model = fin_ref.shape[1]
    taps_cl, chans = in_ref.shape
    wf = d_model // n_tm
    wm = chans // n_tm
    pieces = d_model // chans
    for a in range(n_tm):
        for b in range(n_seq):
            fin_ref[b * er : (b + 1) * er, a * wf : (a + 1) * wf] = gath[a % cores, a // cores, b, :, :wf].astype(F32)
            small[b * er : (b + 1) * er, a * wm : (a + 1) * wm] = gath[a % cores, a // cores, b, :, wf : wf + wm].astype(F32)
    in_ref[...] = small[:taps_cl, :]
    bias_ref[...] = small[taps_cl : taps_cl + 1, :]
    for b in range(2):
        for p in range(pieces):
            at = taps_cl + 1 + b * pieces + p
            mod_ref[b : b + 1, p * chans : (p + 1) * chans] = small[at : at + 1, :]
    wg_out[...] = wg_ref[...]


def local(n_tm, n_seq, latents, hidden, grad_out, conv_in_w, conv_in_b, conv_w, final_w, modulation, clip_start):
    slab, cl, width = latents.shape
    taps, chans = conv_w.shape[:2]
    tokens, d_model = hidden.shape
    rows = chans // (n_tm * n_seq)
    chips = n_tm // CORES
    backward = [(k, k - 1) for k in range(1, n_tm)]
    forward = [(k, k + 1) for k in range(n_tm - 1)]
    lat_prev = lax.ppermute(latents[slab - 4 :], "tm", forward)
    grad_next = lax.ppermute(grad_out[:2], "tm", backward)
    w_in = conv_in_w.transpose(0, 2, 1).reshape(taps * cl, chans)
    bias = conv_in_b.reshape(1, chans)

    def whole(*shape):
        return pl.BlockSpec(shape, lambda t, c: (0,) * len(shape))

    window = [
        pltpu.VMEM((slab + 4, cl, width), BF16),
        pltpu.VMEM((4 * cl, width), BF16),
        pltpu.VMEM((chans, 4 * cl), BF16),
    ]
    w4 = pl.pallas_call(
        weight_kernel,
        out_shape=jax.ShapeDtypeStruct((CORES, chips, n_seq, rows, taps * chans), BF16),
        grid_spec=pltpu.PrefetchScalarGridSpec(
            num_scalar_prefetch=1,
            grid=(slab,),
            in_specs=[
                whole(4, cl, width),
                whole(slab, cl, width),
                pl.BlockSpec((1, chans, width), lambda t, c: (t, 0, 0)),
                whole(taps * cl, chans),
                whole(1, chans),
            ],
            out_specs=whole(CORES, chips, n_seq, rows, taps * chans),
            scratch_shapes=window
            + [pltpu.VMEM((slab + 2, chans, width), BF16), pltpu.VMEM((chans, taps * chans), F32)],
        ),
        compiler_params=pltpu.CompilerParams(vmem_limit_bytes=MAX_VMEM),
        cost_estimate=pl.CostEstimate(flops=7 * 10**9, bytes_accessed=6 * 10**6, transcendentals=2 * 10**6),
        name="weight_grad",
    )(clip_start, lat_prev, latents, grad_out, w_in, bias)

    lg, misc = pl.pallas_call(
        latent_kernel,
        out_shape=(
            jax.ShapeDtypeStruct((slab + 2, cl, width), F32),
            jax.ShapeDtypeStruct((4 * cl, chans), F32),
        ),
        grid_spec=pltpu.PrefetchScalarGridSpec(
            num_scalar_prefetch=1,
            grid=(slab,),
            in_specs=[
                whole(4, cl, width),
                whole(slab, cl, width),
                pl.BlockSpec(memory_space=pl.ANY),
                pl.BlockSpec(memory_space=pl.ANY),
                whole(taps * cl, chans),
                whole(1, chans),
                whole(taps, chans, chans),
            ],
            out_specs=(whole(slab + 2, cl, width), whole(4 * cl, chans)),
            scratch_shapes=window
            + [
                pltpu.VMEM((chans, taps * chans), BF16),
                pltpu.VMEM(((slab + 5) * chans, width), BF16),
                pltpu.SemaphoreType.DMA((2,)),
            ],
        ),
        compiler_params=pltpu.CompilerParams(vmem_limit_bytes=MAX_VMEM),
        cost_estimate=pl.CostEstimate(flops=7 * 10**9, bytes_accessed=6 * 10**6, transcendentals=10**6),
        name="latent_grad",
    )(
        clip_start, lat_prev, latents, grad_out.reshape(slab * chans, width),
        grad_next.reshape(2 * chans, width), w_in, bias, conv_w,
    )

    e = cl * PATCH
    er = e // n_seq
    cw = -(-((d_model + chans) // n_tm) // 128) * 128
    vmem = pl.BlockSpec(memory_space=pltpu.VMEM)
    dma = pltpu.SemaphoreType.DMA
    nt, ns = chips - 1, n_seq - 1
    dx, wg, gath = pl.pallas_call(
        functools.partial(token_kernel, n_tm, n_seq),
        out_shape=(
            jax.ShapeDtypeStruct((tokens, d_model), BF16),
            jax.ShapeDtypeStruct((taps, rows, chans), F32),
            jax.ShapeDtypeStruct((CORES, chips, n_seq, er, cw), BF16),
        ),
        in_specs=[vmem] * 6,
        out_specs=(vmem,) * 3,
        scratch_shapes=[
            pltpu.VMEM((n_seq, cl, width), F32),
            pltpu.VMEM((n_seq, cl, width), F32),
            pltpu.VMEM((tokens, e), BF16),
            pltpu.VMEM((e, 128), F32),
            pltpu.VMEM((e, d_model), F32),
            pltpu.VMEM((8, d_model), F32),
            pltpu.VMEM((chips, n_seq, rows, taps * chans), BF16),
            pltpu.VMEM((chips, n_seq, rows, taps * chans), BF16),
            pltpu.VMEM((nt, n_seq, rows, taps * chans), BF16),
            pltpu.VMEM((n_seq, rows, taps * chans), BF16),
            pltpu.VMEM((ns, rows, taps * chans), BF16),
            pltpu.VMEM((CORES, chips, n_seq, er, cw), BF16),
            pltpu.VMEM((chips, n_seq, er, cw), BF16),
            pltpu.VMEM((chips, n_seq, er, cw), BF16),
            pltpu.VMEM((nt, n_seq, er, cw), BF16),
            pltpu.VMEM((n_seq, er, cw), BF16),
            pltpu.VMEM((ns, er, cw), BF16),
            dma((ns,)), dma((ns,)), dma((2,)), dma((n_seq,)),
            dma((nt,)), dma((nt,)), dma((ns,)), dma((ns,)),
            dma((nt,)), dma((nt,)), dma((ns,)), dma((ns,)),
            dma((ns,)), dma((ns,)), dma((nt,)), dma((nt,)),
            dma((3,)), dma((3,)),
        ],
        compiler_params=pltpu.CompilerParams(
            vmem_limit_bytes=MAX_VMEM, collective_id=0, has_side_effects=True
        ),
        name="token_grad",
    )(lg, hidden, final_w.T, modulation, w4, misc)
    fin, mod, w_in_grad, bias_grad, wg = pl.pallas_call(
        unpack_kernel,
        out_shape=(
            jax.ShapeDtypeStruct((e, d_model), F32),
            jax.ShapeDtypeStruct((2, d_model), F32),
            jax.ShapeDtypeStruct((taps * cl, chans), F32),
            jax.ShapeDtypeStruct((1, chans), F32),
            jax.ShapeDtypeStruct((taps, rows, chans), F32),
        ),
        in_specs=[vmem] * 2,
        out_specs=(vmem,) * 5,
        scratch_shapes=[pltpu.VMEM((e, chans), F32)],
        name="unpack",
    )(gath, wg)
    return (
        dx,
        wg.transpose(1, 0, 2),
        w_in_grad.reshape(taps, cl, chans).transpose(0, 2, 1),
        bias_grad.reshape(chans),
        fin.T,
        mod,
    )


def solution(mesh):
    return jax.shard_map(
        functools.partial(local, mesh.shape["tm"], mesh.shape["seq"]),
        mesh=mesh,
        in_specs=(
            P("tm", None, "seq"),
            P(("tm", "seq"), None),
            P("tm", None, "seq"),
            P(),
            P(),
            P(),
            P(),
            P(),
            P(),
        ),
        out_specs=(P(("tm", "seq"), None), P(("tm", "seq"), None, None), P(), P(), P(), P()),
        check_vma=False,
    )
```

```python
import functools

import jax
import jax.numpy as jnp
from jax import lax
from jax.experimental import pallas as pl
from jax.experimental.pallas import tpu as pltpu
from jax.sharding import PartitionSpec as P

F32 = jnp.float32
BF16 = jnp.bfloat16
MESH = pl.DeviceIdType.MESH
PATCH = 4
CORES = 2
MAX_VMEM = 60 * 1024 * 1024


def dot(a, b, ca, cb):
    return lax.dot_general(a, b, (((ca,), (cb,)), ((), ())), preferred_element_type=F32)


def load_in_weights(w_in_ref, b_ref, w64):
    bias = b_ref[...]
    hi = bias.astype(BF16)
    mid = (bias - hi.astype(F32)).astype(BF16)
    lo = (bias - hi.astype(F32) - mid.astype(F32)).astype(BF16)
    pad = jnp.zeros((16 - 3, bias.shape[1]), F32)
    rows = jnp.concatenate(
        [w_in_ref[...].astype(F32), hi.astype(F32), mid.astype(F32), lo.astype(F32), pad], axis=0
    )
    w64[...] = rows.T.astype(BF16)


def load_window(prev_ref, lat_ref, latx):
    latx[: prev_ref.shape[0]] = prev_ref[...]
    latx[prev_ref.shape[0] :] = lat_ref[...]


def source(clip_ref, frame, tap):
    frames = clip_ref.shape[0]
    return jnp.maximum(frame - tap, clip_ref[jnp.clip(frame, 0, frames - 1)])


def pre_of(clip_ref, latx, z, w64, frame, base):
    cl = latx.shape[1]
    top = latx.shape[0] - 1
    for tap in range(3):
        row = jnp.clip(source(clip_ref, frame, tap) - base, 0, top)
        z[tap * cl : (tap + 1) * cl] = latx[row]
    z[3 * cl :] = jnp.ones_like(z[3 * cl :])
    return dot(w64[...], z[...], 1, 0)


def sigmoid(x):
    return 0.5 * jnp.tanh(0.5 * x) + 0.5


def weight_kernel(clip_ref, prev_ref, lat_ref, grad_ref, w_in_ref, b_ref, out_ref, latx, z, w64, act, acc):
    step = pl.program_id(0)
    slab = lat_ref.shape[0]
    halo = prev_ref.shape[0]
    chans = grad_ref.shape[1]
    first = lax.axis_index("tm") * slab

    def activate(frame):
        pre = pre_of(clip_ref, latx, z, w64, frame, first - halo)
        act[frame - first + 2] = (pre * sigmoid(pre)).astype(BF16)

    @pl.when(step == 0)
    def _():
        load_in_weights(w_in_ref, b_ref, w64)
        load_window(prev_ref, lat_ref, latx)
        acc[...] = jnp.zeros_like(acc)

    @pl.loop(jnp.where(step == 0, -2, step), step + 1)
    def _(t):
        activate(first + t)

    grad = grad_ref[0]
    for tap in range(3):
        row = source(clip_ref, first + step, tap) - first + 2
        acc[:, tap * chans : (tap + 1) * chans] += dot(grad, act[row], 1, 1)

    @pl.when(step == slab - 1)
    def _():
        cores, chips, n_seq, rows, _ = out_ref.shape
        for i in range(cores * chips):
            for j in range(n_seq):
                at = (i * n_seq + j) * rows
                out_ref[i % cores, i // cores, j] = acc[at : at + rows, :].astype(BF16)


def latent_kernel(
    clip_ref, prev_ref, lat_ref, grad_ref, next_ref, w_in_ref, b_ref, w_ref,
    lg_ref, misc_ref, latx, z, w64, wt, gx, sem,
):
    step = pl.program_id(0)
    slab = lat_ref.shape[0]
    halo = prev_ref.shape[0]
    chans = w_ref.shape[1]
    cl = lat_ref.shape[1]
    frames = clip_ref.shape[0]
    first = lax.axis_index("tm") * slab

    @pl.when(step == 0)
    def _():
        own = pltpu.make_async_copy(grad_ref, gx.at[pl.ds(0, slab * chans)], sem.at[0])
        own.start()
        following = pltpu.make_async_copy(next_ref, gx.at[pl.ds(slab * chans, 2 * chans)], sem.at[1])
        following.start()
        load_in_weights(w_in_ref, b_ref, w64)
        load_window(prev_ref, lat_ref, latx)
        for tap in range(3):
            wt[:, tap * chans : (tap + 1) * chans] = w_ref[tap].T
        lg_ref[...] = jnp.zeros_like(lg_ref)
        misc_ref[...] = jnp.zeros_like(misc_ref)
        own.wait()
        following.wait()

    s = first + step
    spare = (slab + 2) * chans

    def start_of(frame):
        return jnp.where(frame < frames, clip_ref[jnp.minimum(frame, frames - 1)], frames)

    a1 = start_of(s + 1) <= s
    a2 = start_of(s + 2) <= s
    b0 = start_of(s) == s
    b1 = start_of(s + 1) == s
    plain = a1 & a2 & jnp.logical_not(b0) & jnp.logical_not(b1)

    @pl.when(jnp.logical_not(plain))
    def _():
        g0 = gx[pl.ds(pl.multiple_of(step * chans, chans), chans)]
        g1 = gx[pl.ds(pl.multiple_of((step + 1) * chans, chans), chans)].astype(F32)
        g2 = gx[pl.ds(pl.multiple_of((step + 2) * chans, chans), chans)].astype(F32)
        gf = g0.astype(F32)
        m = [jnp.where(c, 1.0, 0.0).astype(F32) for c in (a1, a2, b0, b1)]
        gx[spare : spare + chans] = g0
        gx[spare + chans : spare + 2 * chans] = (m[0] * g1 + m[2] * gf).astype(BF16)
        gx[spare + 2 * chans : spare + 3 * chans] = (m[1] * g2 + m[3] * g1 + m[2] * gf).astype(BF16)

    at = pl.multiple_of(jnp.where(plain, step * chans, spare), chans)
    grad_act = dot(wt[...], gx[pl.ds(at, 3 * chans)], 1, 0)
    pre = pre_of(clip_ref, latx, z, w64, s, first - halo)
    sig = sigmoid(pre)
    grad_pre = (grad_act * (sig * (1.0 + pre * (1.0 - sig)))).astype(BF16)
    misc_ref[...] += dot(z[...], grad_pre, 1, 1)
    parts = dot(w_in_ref[...], grad_pre, 1, 0)
    for tap in range(3):
        row = source(clip_ref, s, tap) - first + 2
        lg_ref[row] += parts[tap * cl : (tap + 1) * cl]


def token_kernel(
    n_tm, n_seq,
    lg_ref, hid_hbm, fw_ref, modu_ref, w4_ref, misc_ref,
    dx_hbm, wg_ref, gath,
    hid_ref, dx_ref, s_hid, s_dx, tok, tok_halo, tgs, tcol, facc, macc, wcore, whalf, wrecv, wsum, wrecv2, f4, fcore, fhalf, frecv, fsum, frecv2,
    s_tok, r_tok, s_halo, r_halo, s_w, r_w, s_w2, r_w2, s_f, r_f, s_f2, r_f2, s_g, r_g, s_g2, r_g2, s_core, r_core,
):
    i = lax.axis_index("tm")
    j = lax.axis_index("seq")
    chips = n_tm // CORES
    core = lax.rem(i, CORES)
    chip = lax.div(i, CORES)
    other = CORES - 1 - core
    sibling = (chip * CORES + other, j)
    tms = [(d, lax.rem(chip + d, chips)) for d in range(1, chips)]
    seqs = [(d, lax.rem(j + d, n_seq)) for d in range(1, n_seq)]
    cl = lg_ref.shape[1]
    width = lg_ref.shape[2]
    d_model = hid_ref.shape[1]
    hid_copy = pltpu.make_async_copy(hid_hbm, hid_ref, s_hid)
    hid_copy.start()
    takes_halo = (i < n_tm - 1) & (j >= n_seq - 2)

    barrier = pltpu.get_barrier_semaphore()
    for _, p in tms:
        pl.semaphore_signal(barrier, inc=1, device_id=(p * CORES + core, j), device_id_type=MESH)
    pl.semaphore_signal(barrier, inc=1, device_id=sibling, device_id_type=MESH)
    for _, p in seqs:
        pl.semaphore_signal(barrier, inc=1, device_id=(i, p), device_id_type=MESH)

    @pl.when(j >= n_seq - 2)
    def _():
        for p in range(n_seq):
            pl.semaphore_signal(barrier, inc=1, device_id=(lax.rem(i + 1, n_tm), p), device_id_type=MESH)

    pl.semaphore_wait(barrier, chips + n_seq + 1)

    def copy(src, dst, send, recv, to):
        return pltpu.make_async_remote_copy(
            src_ref=src, dst_ref=dst, send_sem=send, recv_sem=recv, device_id=to, device_id_type=MESH
        )

    tok_copies = [
        copy(lg_ref.at[2 + p], tok.at[j], s_tok.at[d - 1], r_tok.at[d - 1], (i, p)) for d, p in seqs
    ]

    def halo_copy(h):
        return copy(lg_ref.at[h], tok_halo.at[j], s_halo.at[h], r_halo.at[j], (i - 1, n_seq - 2 + h))

    for c in tok_copies:
        c.start()

    @pl.when(i > 0)
    def _():
        for h in range(2):
            halo_copy(h).start()

    w_core = copy(w4_ref.at[other], wcore, s_core.at[0], r_core.at[0], sibling)
    w_core.start()

    @pl.when(jnp.logical_not(takes_halo))
    def _():
        tok_halo[...] = jnp.zeros_like(tok_halo)

    n = width // PATCH
    row = lax.broadcasted_iota(jnp.int32, (width, width), 0)
    col = lax.broadcasted_iota(jnp.int32, (width, width), 1)
    spread = jnp.where(row == lax.rem(col, n) * PATCH + lax.div(col, n), 1.0, 0.0).astype(BF16)
    e = cl * PATCH
    row = lax.broadcasted_iota(jnp.int32, (e, e), 0)
    col = lax.broadcasted_iota(jnp.int32, (e, e), 1)
    order = jnp.where(row == lax.rem(col, cl) * PATCH + lax.div(col, cl), 1.0, 0.0).astype(BF16)

    facc[...] = jnp.zeros_like(facc)
    tcol[...] = jnp.zeros_like(tcol)
    w_core.wait()
    for q in range(chips):
        whalf[q] = (w4_ref[core, q].astype(F32) + wcore[q].astype(F32)).astype(BF16)
    w_copies = [
        copy(whalf.at[p], wrecv.at[d - 1], s_w.at[d - 1], r_w.at[d - 1], (p * CORES + core, j))
        for d, p in tms
    ]
    for c in w_copies:
        c.start()
    for c in tok_copies:
        c.wait()

    @pl.when(i > 0)
    def _():
        for h in range(2):
            halo_copy(h).wait_send()

    @pl.when(takes_halo)
    def _():
        for p in range(n_seq):
            copy(lg_ref.at[0], tok_halo.at[p], s_halo.at[0], r_halo.at[p], (i, j)).wait_recv()

    tok[j] = lg_ref[2 + j]

    shift = modu_ref[0:1, :]
    scale = 1.0 + modu_ref[1:2, :]

    def rows_of(r):
        return pl.ds(pl.multiple_of(r * n, n), n)

    def normalise(r):
        hid = hid_ref[rows_of(r), :].astype(F32)
        center = hid - jnp.mean(hid, axis=1, keepdims=True)
        inv = lax.rsqrt(jnp.mean(center * center, axis=1, keepdims=True) + 1e-06)
        return center * inv, inv

    hid_copy.wait()

    @pl.loop(0, n_seq)
    def _(r):
        lat = (tok[r] + tok_halo[r]).astype(BF16)
        split = dot(lat, spread, 1, 0)
        stack = jnp.concatenate([split[:, q * n : (q + 1) * n] for q in range(PATCH)], axis=0)
        tg_t = dot(order, stack.astype(BF16), 1, 0)
        tgs[rows_of(r), :] = tg_t.T.astype(BF16)
        normed, _ = normalise(r)
        facc[...] += dot(tg_t.astype(BF16), normed.astype(BF16), 1, 0)
        tcol[...] += jnp.broadcast_to(jnp.sum(tg_t, axis=1, keepdims=True), tcol.shape)

    column = tcol[:, 0:1]
    fw = fw_ref[...].astype(F32)
    macc[0:1] = jnp.sum(fw * column, axis=0, keepdims=True)
    macc[1:2] = jnp.sum(fw * facc[...], axis=0, keepdims=True)
    facc[...] = facc[...] * scale + column * shift

    chans = misc_ref.shape[1]
    wf = d_model // n_tm
    wm = chans // n_tm
    er = e // n_seq
    pieces = d_model // chans
    small = jnp.concatenate(
        [misc_ref[0 : 3 * cl + 1, :]]
        + [macc[b : b + 1, p * chans : (p + 1) * chans] for b in range(2) for p in range(pieces)]
        + [jnp.zeros((e - 3 * cl - 1 - 2 * pieces, chans), F32)],
        axis=0,
    )
    for a in range(n_tm):
        for b in range(n_seq):
            f4[a % CORES, a // CORES, b, :, :wf] = facc[b * er : (b + 1) * er, a * wf : (a + 1) * wf].astype(BF16)
            f4[a % CORES, a // CORES, b, :, wf : wf + wm] = small[b * er : (b + 1) * er, a * wm : (a + 1) * wm].astype(BF16)
            if wf + wm < f4.shape[4]:
                f4[a % CORES, a // CORES, b, :, wf + wm :] = jnp.zeros((er, f4.shape[4] - wf - wm), BF16)
    f_core = copy(f4.at[other], fcore, s_core.at[1], r_core.at[1], sibling)
    f_core.start()

    def input_gradient(r):
        normed, inv = normalise(r)
        ng = dot(tgs[rows_of(r), :], fw_ref[...], 1, 0) * scale
        m1 = jnp.mean(ng, axis=1, keepdims=True)
        m2 = jnp.mean(ng * normed, axis=1, keepdims=True)
        dx_ref[rows_of(r), :] = (inv * (ng - m1 - normed * m2)).astype(BF16)

    pl.loop(0, n_seq // 2)(input_gradient)
    f_core.wait()
    for q in range(chips):
        fhalf[q] = (f4[core, q].astype(F32) + fcore[q].astype(F32)).astype(BF16)
    f_copies = [
        copy(fhalf.at[p], frecv.at[d - 1], s_f.at[d - 1], r_f.at[d - 1], (p * CORES + core, j))
        for d, p in tms
    ]
    for c in f_copies:
        c.start()
    pl.loop(n_seq // 2, n_seq)(input_gradient)
    dx_copy = pltpu.make_async_copy(dx_ref, dx_hbm, s_dx)
    dx_copy.start()

    for c in w_copies:
        c.wait()
    for b in range(n_seq):
        total = whalf[chip, b].astype(F32)
        for k in range(chips - 1):
            total = total + wrecv[k, b].astype(F32)
        wsum[b] = total.astype(BF16)
    w2_copies = [
        copy(wsum.at[p], wrecv2.at[d - 1], s_w2.at[d - 1], r_w2.at[d - 1], (i, p)) for d, p in seqs
    ]
    for c in w2_copies:
        c.start()

    for c in f_copies:
        c.wait()
    total = fhalf[chip].astype(F32)
    for k in range(chips - 1):
        total = total + frecv[k].astype(F32)
    fsum[...] = total.astype(BF16)
    f2_copies = [
        copy(fsum.at[p], frecv2.at[d - 1], s_f2.at[d - 1], r_f2.at[d - 1], (i, p)) for d, p in seqs
    ]
    for c in f2_copies:
        c.start()

    for c in w2_copies:
        c.wait()
    total = wsum[j].astype(F32)
    for k in range(n_seq - 1):
        total = total + wrecv2[k].astype(F32)
    for tap in range(3):
        wg_ref[tap] = total[:, tap * chans : (tap + 1) * chans]

    for c in f2_copies:
        c.wait()
    total = fsum[j].astype(F32)
    for k in range(n_seq - 1):
        total = total + frecv2[k].astype(F32)
    gath[core, chip, j] = total.astype(BF16)
    g_copies = [
        copy(gath.at[core, chip, j], gath.at[core, chip, j], s_g.at[d - 1], r_g.at[d - 1], (i, p)) for d, p in seqs
    ]
    for c in g_copies:
        c.start()
    for c in g_copies:
        c.wait()
    g2_copies = [
        copy(gath.at[core, chip], gath.at[core, chip], s_g2.at[d - 1], r_g2.at[d - 1], (p * CORES + core, j))
        for d, p in tms
    ]
    for c in g2_copies:
        c.start()
    for c in g2_copies:
        c.wait()
    g_core = copy(gath.at[core], gath.at[core], s_core.at[2], r_core.at[2], sibling)
    g_core.start()
    g_core.wait()
    dx_copy.wait()


def unpack_kernel(gath, wg_ref, fin_ref, mod_ref, in_ref, bias_ref, wg_out, small):
    cores, chips, n_seq, er, _ = gath.shape
    n_tm = cores * chips
    d_model = fin_ref.shape[1]
    taps_cl, chans = in_ref.shape
    wf = d_model // n_tm
    wm = chans // n_tm
    pieces = d_model // chans
    for a in range(n_tm):
        for b in range(n_seq):
            fin_ref[b * er : (b + 1) * er, a * wf : (a + 1) * wf] = gath[a % cores, a // cores, b, :, :wf].astype(F32)
            small[b * er : (b + 1) * er, a * wm : (a + 1) * wm] = gath[a % cores, a // cores, b, :, wf : wf + wm].astype(F32)
    in_ref[...] = small[:taps_cl, :]
    bias_ref[...] = small[taps_cl : taps_cl + 1, :]
    for b in range(2):
        for p in range(pieces):
            at = taps_cl + 1 + b * pieces + p
            mod_ref[b : b + 1, p * chans : (p + 1) * chans] = small[at : at + 1, :]
    wg_out[...] = wg_ref[...]


def local(n_tm, n_seq, latents, hidden, grad_out, conv_in_w, conv_in_b, conv_w, final_w, modulation, clip_start):
    slab, cl, width = latents.shape
    taps, chans = conv_w.shape[:2]
    tokens, d_model = hidden.shape
    rows = chans // (n_tm * n_seq)
    chips = n_tm // CORES
    backward = [(k, k - 1) for k in range(1, n_tm)]
    forward = [(k, k + 1) for k in range(n_tm - 1)]
    lat_prev = lax.ppermute(latents[slab - 4 :], "tm", forward)
    grad_next = lax.ppermute(grad_out[:2], "tm", backward)
    w_in = conv_in_w.transpose(0, 2, 1).reshape(taps * cl, chans)
    bias = conv_in_b.reshape(1, chans)

    def whole(*shape):
        return pl.BlockSpec(shape, lambda t, c: (0,) * len(shape))

    window = [
        pltpu.VMEM((slab + 4, cl, width), BF16),
        pltpu.VMEM((4 * cl, width), BF16),
        pltpu.VMEM((chans, 4 * cl), BF16),
    ]
    w4 = pl.pallas_call(
        weight_kernel,
        out_shape=jax.ShapeDtypeStruct((CORES, chips, n_seq, rows, taps * chans), BF16),
        grid_spec=pltpu.PrefetchScalarGridSpec(
            num_scalar_prefetch=1,
            grid=(slab,),
            in_specs=[
                whole(4, cl, width),
                whole(slab, cl, width),
                pl.BlockSpec((1, chans, width), lambda t, c: (t, 0, 0)),
                whole(taps * cl, chans),
                whole(1, chans),
            ],
            out_specs=whole(CORES, chips, n_seq, rows, taps * chans),
            scratch_shapes=window
            + [pltpu.VMEM((slab + 2, chans, width), BF16), pltpu.VMEM((chans, taps * chans), F32)],
        ),
        compiler_params=pltpu.CompilerParams(vmem_limit_bytes=MAX_VMEM),
        cost_estimate=pl.CostEstimate(flops=7 * 10**9, bytes_accessed=6 * 10**6, transcendentals=2 * 10**6),
        name="weight_grad",
    )(clip_start, lat_prev, latents, grad_out, w_in, bias)

    lg, misc = pl.pallas_call(
        latent_kernel,
        out_shape=(
            jax.ShapeDtypeStruct((slab + 2, cl, width), F32),
            jax.ShapeDtypeStruct((4 * cl, chans), F32),
        ),
        grid_spec=pltpu.PrefetchScalarGridSpec(
            num_scalar_prefetch=1,
            grid=(slab,),
            in_specs=[
                whole(4, cl, width),
                whole(slab, cl, width),
                pl.BlockSpec(memory_space=pl.ANY),
                pl.BlockSpec(memory_space=pl.ANY),
                whole(taps * cl, chans),
                whole(1, chans),
                whole(taps, chans, chans),
            ],
            out_specs=(whole(slab + 2, cl, width), whole(4 * cl, chans)),
            scratch_shapes=window
            + [
                pltpu.VMEM((chans, taps * chans), BF16),
                pltpu.VMEM(((slab + 5) * chans, width), BF16),
                pltpu.SemaphoreType.DMA((2,)),
            ],
        ),
        compiler_params=pltpu.CompilerParams(vmem_limit_bytes=MAX_VMEM),
        cost_estimate=pl.CostEstimate(flops=7 * 10**9, bytes_accessed=6 * 10**6, transcendentals=10**6),
        name="latent_grad",
    )(
        clip_start, lat_prev, latents, grad_out.reshape(slab * chans, width),
        grad_next.reshape(2 * chans, width), w_in, bias, conv_w,
    )

    e = cl * PATCH
    er = e // n_seq
    cw = -(-((d_model + chans) // n_tm) // 128) * 128
    vmem = pl.BlockSpec(memory_space=pltpu.VMEM)
    dma = pltpu.SemaphoreType.DMA
    nt, ns = chips - 1, n_seq - 1
    dx, wg, gath = pl.pallas_call(
        functools.partial(token_kernel, n_tm, n_seq),
        out_shape=(
            jax.ShapeDtypeStruct((tokens, d_model), BF16),
            jax.ShapeDtypeStruct((taps, rows, chans), F32),
            jax.ShapeDtypeStruct((CORES, chips, n_seq, er, cw), BF16),
        ),
        in_specs=[vmem, pl.BlockSpec(memory_space=pl.ANY)] + [vmem] * 4,
        out_specs=(pl.BlockSpec(memory_space=pl.ANY), vmem, vmem),
        scratch_shapes=[
            pltpu.VMEM((tokens, d_model), BF16),
            pltpu.VMEM((tokens, d_model), BF16),
            dma(()),
            dma(()),
            pltpu.VMEM((n_seq, cl, width), F32),
            pltpu.VMEM((n_seq, cl, width), F32),
            pltpu.VMEM((tokens, e), BF16),
            pltpu.VMEM((e, 128), F32),
            pltpu.VMEM((e, d_model), F32),
            pltpu.VMEM((8, d_model), F32),
            pltpu.VMEM((chips, n_seq, rows, taps * chans), BF16),
            pltpu.VMEM((chips, n_seq, rows, taps * chans), BF16),
            pltpu.VMEM((nt, n_seq, rows, taps * chans), BF16),
            pltpu.VMEM((n_seq, rows, taps * chans), BF16),
            pltpu.VMEM((ns, rows, taps * chans), BF16),
            pltpu.VMEM((CORES, chips, n_seq, er, cw), BF16),
            pltpu.VMEM((chips, n_seq, er, cw), BF16),
            pltpu.VMEM((chips, n_seq, er, cw), BF16),
            pltpu.VMEM((nt, n_seq, er, cw), BF16),
            pltpu.VMEM((n_seq, er, cw), BF16),
            pltpu.VMEM((ns, er, cw), BF16),
            dma((ns,)), dma((ns,)), dma((2,)), dma((n_seq,)),
            dma((nt,)), dma((nt,)), dma((ns,)), dma((ns,)),
            dma((nt,)), dma((nt,)), dma((ns,)), dma((ns,)),
            dma((ns,)), dma((ns,)), dma((nt,)), dma((nt,)),
            dma((3,)), dma((3,)),
        ],
        compiler_params=pltpu.CompilerParams(
            vmem_limit_bytes=MAX_VMEM, collective_id=0, has_side_effects=True
        ),
        name="token_grad",
    )(lg, hidden, final_w.T, modulation, w4, misc)
    fin, mod, w_in_grad, bias_grad, wg = pl.pallas_call(
        unpack_kernel,
        out_shape=(
            jax.ShapeDtypeStruct((e, d_model), F32),
            jax.ShapeDtypeStruct((2, d_model), F32),
            jax.ShapeDtypeStruct((taps * cl, chans), F32),
            jax.ShapeDtypeStruct((1, chans), F32),
            jax.ShapeDtypeStruct((taps, rows, chans), F32),
        ),
        in_specs=[vmem] * 2,
        out_specs=(vmem,) * 5,
        scratch_shapes=[pltpu.VMEM((e, chans), F32)],
        name="unpack",
    )(gath, wg)
    return (
        dx,
        wg.transpose(1, 0, 2),
        w_in_grad.reshape(taps, cl, chans).transpose(0, 2, 1),
        bias_grad.reshape(chans),
        fin.T,
        mod,
    )


def solution(mesh):
    return jax.shard_map(
        functools.partial(local, mesh.shape["tm"], mesh.shape["seq"]),
        mesh=mesh,
        in_specs=(
            P("tm", None, "seq"),
            P(("tm", "seq"), None),
            P("tm", None, "seq"),
            P(),
            P(),
            P(),
            P(),
            P(),
            P(),
        ),
        out_specs=(P(("tm", "seq"), None), P(("tm", "seq"), None, None), P(), P(), P(), P()),
        check_vma=False,
    )
```
